256 devices in a mesh: gx: 8 (over y_lo, x), gy: 32 (over z, y_hi, core).
Axes of the slice: x: 4, y: 4 (y_hi: 2, y_lo: 2; y = y_hi * 2 + y_lo), z: 8, core: 2. Of those that a mesh axis runs over, the one named last changes fastest.
Arguments:
- adjoint_source: float32 [2, 128, 256, 128], P(None, 'gx', 'gy'), may hold values from -16 to 16
- storage: float32 [4, 128, 256, 128], P(None, 'gx', 'gy'), may hold values from -0.2 to 2, as said below
- soil_ids: int32 [128, 256, 128], P('gx', 'gy'), may hold values from 0 to 15
- bc_mask: int32 [128, 256], P('gx', 'gy'), may hold values 0 or 1
- soil_props: float32 [3, 16], replicated, may hold values from 0.1 to 1
Outputs:
- adjoint: float32 [2, 128, 256, 128], P(None, 'gx', 'gy')
- residual: float32 [2, 128, 256, 128], P(None, 'gx', 'gy')
- next_basis: float32 [2, 128, 256, 128], P(None, 'gx', 'gy')
The draws below stay inside these ranges and needn't reach their ends.
Inputs may be any that keep to these rules, and one draw needn't show every extreme that they name: `storage`: sp and St lie in 0.2 to 2, Spt within -0.04 to 0.04, Stp within -0.2 to 0.2.
All inputs are finite; a program needn't handle non-finite values. No bound on the sum of `bc_mask` on one device may be relied on, other than what follows from the above.
Results may differ from the reference program's by a relative error of at most 0.0008.
Values sent between devices are 32-bit elements; how exact they have to be, the bound alone decides.
A program may use at most 64 MiB of HBM per device.

```python
import math
import jax
import jax.numpy as jnp
from jax import lax

CX = 16
CY = 8
NZ = 128
NMAT = 16
MARGIN = 4
SWEEPS = 6
ITERS = 2
NX = 128
NY = 256
N_GX = 8
N_GY = 32


def draw_storage(key, part):
    keys = jax.random.split(key, 4)
    shape = (NX, NY, NZ)
    diag_press = jnp.exp(jax.random.uniform(keys[0], shape, jnp.float32, math.log(0.2), math.log(2.0)))
    diag_heat = jnp.exp(jax.random.uniform(keys[1], shape, jnp.float32, math.log(0.2), math.log(2.0)))
    cross_pt = jax.random.uniform(keys[2], shape, jnp.float32, -0.04, 0.04)
    cross_tp = jax.random.uniform(keys[3], shape, jnp.float32, -0.2, 0.2)
    return jnp.stack([diag_press, cross_pt, cross_tp, diag_heat])


def draw_adjoint_source(key, part):
    shape = (2, NX, NY, NZ)
    ramp_x = jnp.arange(NX, dtype=jnp.float32) / (NX - 1)
    ramp_y = jnp.arange(NY, dtype=jnp.float32) / (NY - 1)
    level = ramp_x[:, None] + ramp_y[None, :] - 1.0
    amplitude = jnp.exp(math.log(3.0) * level)[None, :, :, None]
    noise = jnp.clip(jax.random.normal(key, shape, jnp.float32), -4.0, 4.0)
    return amplitude * noise


def set_ends(values, own_key, low, largest):
    shape = values.shape
    spot = [jax.random.randint(jax.random.fold_in(own_key, axis), (), 0, shape[axis]) for axis in range(len(shape))]
    values = values.at[tuple(spot)].set(low)
    longest = shape.index(max(shape))
    spot[longest] = (spot[longest] + 1) % shape[longest]
    return values.at[tuple(spot)].set(largest)


def setup_inputs(seed: int = 0) -> dict:
    seeds = jax.random.split(jax.random.key(seed), 6)
    adjoint_source = draw_adjoint_source(jax.random.fold_in(seeds[5], 71), 0)
    storage = draw_storage(jax.random.fold_in(seeds[5], 71), 0)
    soil_ids = set_ends(jax.random.randint(seeds[2], (NX, NY, NZ), 0, NMAT), jax.random.fold_in(seeds[2], 1), 0, NMAT - 1).astype(jnp.int32)
    bc_mask = set_ends((jax.random.randint(seeds[3], (NX, NY), 0, 2) < 1).astype(jnp.int32), jax.random.fold_in(seeds[3], 1), 0, 1)
    soil_props = jnp.clip(jnp.exp(jax.random.uniform(seeds[4], (3, NMAT), jnp.float32, math.log(0.1), math.log(1.0))), 0.1, 1.0)
    return {"adjoint_source": adjoint_source, "storage": storage, "soil_ids": soil_ids, "bc_mask": bc_mask, "soil_props": soil_props}


epsilon = 1e-06

def neighbour_list(field):
    middle = field[1:-1, 1:-1]
    below = jnp.pad(middle[:, :, :-1], ((0, 0), (0, 0), (1, 0)))
    above = jnp.pad(middle[:, :, 1:], ((0, 0), (0, 0), (0, 1)))
    return [field[:-2, 1:-1], field[2:, 1:-1], field[1:-1, :-2], field[1:-1, 2:], below, above]

def face_parts(coefficients):
    centre = coefficients[:, 1:-1, 1:-1]
    press_faces = jnp.stack([jnp.sqrt(centre[0] * other) for other in neighbour_list(coefficients[0])])
    heat_faces = jnp.stack([jnp.sqrt(centre[1] * other) for other in neighbour_list(coefficients[1])])
    return (press_faces, heat_faces, centre)

def laplace(field, faces, diagonal):
    total = diagonal * field[1:-1, 1:-1]
    for index, other in enumerate(neighbour_list(field)):
        total = total - faces[index] * other
    return total

def apply_adjoint(padded, spread_e, press_faces, heat_faces, centre):
    press_part = padded[0]
    heat_part = padded[1]
    mixed = press_part + spread_e * heat_part
    press_diag = lax.optimization_barrier(jnp.sum(press_faces, axis=0)) + centre[7]
    heat_diag = lax.optimization_barrier(jnp.sum(heat_faces, axis=0))
    press_mid = press_part[1:-1, 1:-1]
    heat_mid = heat_part[1:-1, 1:-1]
    press_out = centre[3] * press_mid + laplace(mixed, press_faces, press_diag) + centre[5] * heat_mid
    heat_out = centre[4] * press_mid + centre[6] * heat_mid + laplace(heat_part, heat_faces, heat_diag)
    return jnp.stack([press_out, heat_out])

def block_inverse(press_faces, heat_faces, centre, outside):
    press_diag = lax.optimization_barrier(jnp.sum(press_faces, axis=0)) + centre[7]
    heat_diag = lax.optimization_barrier(jnp.sum(heat_faces, axis=0))
    first = centre[3] + press_diag + outside
    cross = centre[5] + centre[2] * press_diag
    lower = centre[4]
    last = centre[6] + heat_diag + outside
    determinant = first * last - cross * lower
    return (last / determinant, -cross / determinant, -lower / determinant, first / determinant)

def subdomain_solve(rhs, press_faces, heat_faces, centre, inverse, spread_e):
    solution = jnp.zeros_like(rhs)
    for sweep in range(SWEEPS):
        padded = jnp.pad(solution, ((0, 0), (1, 1), (1, 1), (0, 0)))
        remain = rhs - apply_adjoint(padded, spread_e, press_faces, heat_faces, centre)
        step_p = inverse[0] * remain[0] + inverse[1] * remain[1]
        step_t = inverse[2] * remain[0] + inverse[3] * remain[1]
        solution = solution + jnp.stack([step_p, step_t])
    return solution

def assemble(material, storage, bc_mask):
    depth = material.shape[3]
    top = lax.broadcasted_iota(jnp.int32, (1, 1, depth), 2) == depth - 1
    boundary = jnp.where(top, 2.0 * material[0] * bc_mask[:, :, None].astype(jnp.float32), 0.0)
    return jnp.concatenate([material, storage, boundary[None]], axis=0)

def least_squares(columns, beta):
    count = len(columns)
    target = [beta] + [0.0 * beta for index in range(count)]
    rotations = []
    upper = []
    for column_index, column in enumerate(columns):
        values = list(column)
        for index, pair in enumerate(rotations):
            high = pair[0] * values[index] + pair[1] * values[index + 1]
            low = -pair[1] * values[index] + pair[0] * values[index + 1]
            values[index] = high
            values[index + 1] = low
        radius = jnp.sqrt(values[column_index] * values[column_index] + values[column_index + 1] * values[column_index + 1])
        cosine = values[column_index] / radius
        sine = values[column_index + 1] / radius
        values[column_index] = radius
        rotations.append((cosine, sine))
        high = cosine * target[column_index] + sine * target[column_index + 1]
        low = -sine * target[column_index] + cosine * target[column_index + 1]
        target[column_index] = high
        target[column_index + 1] = low
        upper.append(values[:column_index + 1])
    weights = [None] * count
    for index in reversed(range(count)):
        accum = target[index]
        for later in range(index + 1, count):
            accum = accum - upper[later][index] * weights[later]
        weights[index] = accum / upper[index][index]
    return weights

def reference(adjoint_source, storage, soil_ids, bc_mask, soil_props):
    material = jnp.take(soil_props, soil_ids, axis=1)
    coefficients = assemble(material, storage, bc_mask)
    cycle = MARGIN + 1
    padded_coeffs = jnp.pad(coefficients, ((0, 0), (cycle, cycle), (cycle, cycle), (0, 0)))
    own_coeffs = padded_coeffs[:, MARGIN:-MARGIN, MARGIN:-MARGIN]
    own_press, own_heat, own_centre = face_parts(own_coeffs)

    def image_of(vector):
        padded = jnp.pad(vector, ((0, 0), (1, 1), (1, 1), (0, 0)))
        return apply_adjoint(padded, own_coeffs[2], own_press, own_heat, own_centre)
    span_x = jnp.arange(CX + 2 * MARGIN, dtype=jnp.int32)
    span_y = jnp.arange(CY + 2 * MARGIN, dtype=jnp.int32)

    def precondition(vector):
        accum = jnp.zeros((2, NX + 2 * MARGIN, NY + 2 * MARGIN, NZ), jnp.float32)

        def one_domain(domain, accum):
            start_x = (domain // N_GY * CX).astype(jnp.int32)
            start_y = (domain % N_GY * CY).astype(jnp.int32)
            zero = jnp.zeros((), jnp.int32)
            local = lax.dynamic_slice(padded_coeffs, (zero, start_x, start_y, zero), (8, CX + 2 * cycle, CY + 2 * cycle, NZ))
            owned = lax.dynamic_slice(vector, (zero, start_x, start_y, zero), (2, CX, CY, NZ))
            rhs = jnp.pad(owned, ((0, 0), (MARGIN, MARGIN), (MARGIN, MARGIN), (0, 0)))
            along_x = start_x - MARGIN + span_x
            along_y = start_y - MARGIN + span_y
            inside_x = (along_x >= 0) & (along_x < NX)
            inside_y = (along_y >= 0) & (along_y < NY)
            outside = (1.0 - (inside_x[:, None] & inside_y[None, :]).astype(jnp.float32))[:, :, None]
            press_faces, heat_faces, centre = face_parts(local)
            inverse = block_inverse(press_faces, heat_faces, centre, outside)
            solved = subdomain_solve(rhs, press_faces, heat_faces, centre, inverse, local[2])
            current = lax.dynamic_slice(accum, (zero, start_x, start_y, zero), solved.shape)
            return lax.dynamic_update_slice(accum, current + solved, (zero, start_x, start_y, zero))
        accum = lax.fori_loop(0, N_GX * N_GY, one_domain, accum)
        return accum[:, MARGIN:-MARGIN, MARGIN:-MARGIN]
    beta = jnp.sqrt(jnp.sum(adjoint_source * adjoint_source) + epsilon)
    basis = [adjoint_source / beta]
    directions = []
    columns = []
    for column_index in range(ITERS):
        direction = precondition(basis[-1])
        directions.append(direction)
        image = image_of(direction)
        heights = [jnp.sum(image * prior) for prior in basis]
        for height, prior in zip(heights, basis):
            image = image - height * prior
        length = jnp.sqrt(jnp.sum(image * image) + epsilon)
        heights.append(length)
        columns.append(heights)
        basis.append(image / length)
    weights = least_squares(columns, beta)
    adjoint = weights[0] * directions[0]
    for index in range(1, ITERS):
        adjoint = adjoint + weights[index] * directions[index]
    residual = jnp.zeros_like(adjoint_source)
    for row in range(ITERS + 1):
        factor = beta if row == 0 else 0.0 * beta
        for column_index in range(ITERS):
            if row <= column_index + 1:
                factor = factor - columns[column_index][row] * weights[column_index]
        residual = residual + factor * basis[row]
    next_basis = basis[-1] * math.sqrt(2.0 * NX * NY * NZ)
    return (adjoint, residual, next_basis)
```

```python
import functools
import math

import jax
import jax.numpy as jnp
from jax import lax
from jax.experimental import pallas as pl
from jax.experimental.pallas import tpu as pltpu
from jax.sharding import PartitionSpec as P

MESH = pl.DeviceIdType.MESH
CX = 16
EX = 26
OWN = 5
SWEEPS = 6
epsilon = 1e-06


SIDES = [(dx, dy) for dy in (1, -1, 0) for dx in (0, 1, -1) if (dx, dy) != (0, 0)]


def planes(low, high, chunk, body):
    count = (high - low) // chunk

    def group(index, carry):
        body(low + index * chunk)
        return carry

    lax.fori_loop(0, count, group, 0)


def ring_sum(left, a, b, right, rows, lanes):
    a_up, b_up = pltpu.roll(a, 7, 0), pltpu.roll(b, 7, 0)
    a_down, b_down = pltpu.roll(a, 1, 0), pltpu.roll(b, 1, 0)
    y_a = jnp.where(rows == 7, b_up, a_up) + jnp.where(rows == 0, b_down, a_down)
    b_high = jnp.where(rows == 7, a_up, jnp.where(rows == 3, 0.0, b_up))
    b_low = jnp.where(rows == 0, a_down, jnp.where(rows == 4, 0.0, b_down))
    y_b = b_high + b_low
    out_a = (left[0] + right[0]) + (y_a + z_sum(a, lanes))
    out_b = (left[1] + right[1]) + (y_b + z_sum(b, lanes))
    return out_a, out_b


def z_sum(tile, lanes):
    below = jnp.where(lanes == 0, 0.0, pltpu.roll(tile, 1, 1))
    above = jnp.where(lanes == 127, 0.0, pltpu.roll(tile, 127, 1))
    return below + above


def total_rows(tile):
    tile = tile + pltpu.roll(tile, 4, 0)
    tile = tile + pltpu.roll(tile, 2, 0)
    return tile + pltpu.roll(tile, 1, 0)


def total_lanes(tile):
    for shift in (64, 32, 16, 8, 4, 2, 1):
        tile = tile + pltpu.roll(tile, shift, 1)
    return tile


def small_problem(gram):
    ss, s1, s2, d11, d12, d22 = [gram[i : i + 1] for i in range(6)]
    square = ss + epsilon
    beta = jnp.sqrt(square)
    g1 = (epsilon - s1) / square
    h11 = 1.0 - g1
    norm1 = (d11 + 2.0 * g1 * s1 + g1 * g1 * ss) / square
    h21 = jnp.sqrt(jnp.maximum(norm1, 0.0) + epsilon)
    al = 1.0 / (beta * h21)
    ga = g1 * al
    h12 = (al * (s1 + s2) + ga * (ss + s1)) / beta
    v22 = al * al * d11 + 2.0 * al * ga * s1 + ga * ga * ss
    e22 = al * (al * d12 + ga * d11) + ga * (al * s2 + ga * s1)
    h22 = v22 + e22
    x3 = al
    x2 = ga + (1.0 - h22) * al
    x1 = (1.0 - h22) * ga - h12 / beta
    norm2 = (
        x3 * x3 * d22
        + x2 * x2 * d11
        + x1 * x1 * ss
        + 2.0 * (x3 * x2 * d12 + x3 * x1 * s2 + x2 * x1 * s1)
    )
    h32 = jnp.sqrt(jnp.maximum(norm2, 0.0) + epsilon)
    r1 = jnp.sqrt(h11 * h11 + h21 * h21)
    c1, n1 = h11 / r1, h21 / r1
    t0, t1 = c1 * beta, -n1 * beta
    u12 = c1 * h12 + n1 * h22
    low = c1 * h22 - n1 * h12
    r2 = jnp.sqrt(low * low + h32 * h32)
    c2 = low / r2
    y2 = c2 * t1 / r2
    y1 = (t0 - u12 * y2) / r1
    f1 = beta - h11 * y1 - h12 * y2
    f2 = -h21 * y1 - h22 * y2
    f3 = -h32 * y2
    a1, a2 = y1 / beta + y2 * ga, y2 * al
    scale = 1.0 / h32
    v31, v32, v33 = x1 * scale, x2 * scale, x3 * scale
    q1 = f1 / beta + f2 * ga + f3 * v31
    q2 = f2 * al + f3 * v32
    q3 = f3 * v33
    return a1, a2, q1, q2, q3, v31, v32, v33


def kernel(
    scale,
    source_hbm, storage_hbm, ids_hbm, bc_ref, props_ref,
    adjoint_ref, residual_ref, next_ref,
    source, sa, sb, ia, inn, ip, ba, bb,
    ga, gb, gn, gp, ea, eb, m, k_own, lap, recip, rhs, z, fold, keep_p, keep_d,
    rya, ryb, rx, rca, rcb, g1, g2,
    local_sem, s1, r1, s2, r2, s3, r3, s4, r4,
):
    gx, gy = lax.axis_index("gx"), lax.axis_index("gy")
    n_gx, n_gy = lax.axis_size("gx"), lax.axis_size("gy")
    rows = lax.broadcasted_iota(jnp.int32, (8, 128), 0)
    lanes = lax.broadcasted_iota(jnp.int32, (8, 128), 1)
    zero = jnp.zeros((8, 128), jnp.float32)

    def device(dx, dy):
        x = lax.rem(gx + (dx + n_gx), n_gx) if dx else gx
        y = lax.rem(gy + (dy + n_gy), n_gy) if dy else gy
        return x, y

    loads = [
        pltpu.make_async_copy(storage_hbm, sa.at[:, OWN : OWN + CX], local_sem.at[0]),
        pltpu.make_async_copy(ids_hbm, ia.at[OWN : OWN + CX], local_sem.at[1]),
        pltpu.make_async_copy(source_hbm, source, local_sem.at[2]),
    ]
    for copy in loads:
        copy.start()

    size1, size2 = n_gx * 2, n_gy // 2
    me1 = gx * 2 + lax.rem(gy, 2)
    me2 = lax.div(gy, 2)

    def partner1(step):
        other = lax.rem(me1 + step, size1)
        return lax.div(other, 2), lax.div(gy, 2) * 2 + lax.rem(other, 2)

    def partner2(step):
        other = lax.rem(me2 + step, size2)
        return gx, other * 2 + lax.rem(gy, 2)

    barrier = pltpu.get_barrier_semaphore()
    for dx, dy in SIDES:
        pl.semaphore_signal(barrier, inc=1, device_id=device(dx, dy), device_id_type=MESH)

    def greet(step, carry):
        pl.semaphore_signal(barrier, inc=1, device_id=partner1(step), device_id_type=MESH)
        return carry

    def greet2(step, carry):
        pl.semaphore_signal(barrier, inc=1, device_id=partner2(step), device_id_type=MESH)
        return carry

    lax.fori_loop(1, size1, greet, 0)
    lax.fori_loop(1, size2, greet2, 0)

    own_bc = jnp.concatenate(
        [bc_ref[...].astype(jnp.float32), jnp.zeros((8, 112), jnp.float32)], axis=1
    )
    ba[1] = own_bc
    for slot in range(2):
        for field in range(2):
            for tile in range(2):
                z[slot, field, tile, 0] = zero
                z[slot, field, tile, EX - 1] = zero
    for field in range(2):
        for p in list(range(0, OWN)) + list(range(OWN + CX, EX)):
            rhs[field, p] = zero

    pl.semaphore_wait(barrier, len(SIDES) + size1 - 1 + size2 - 1)
    loads[1].wait()
    loads[0].wait()

    first = []
    for dx, dy in SIDES:
        if dx == 0:
            ids_x, ids_to = slice(5, 21), slice(5, 21)
            sto_x, sto_to = ids_x, ids_to
        elif dx == 1:
            ids_x, ids_to = slice(16, 21), slice(0, 5)
            sto_x, sto_to = slice(17, 21), slice(1, 5)
        else:
            ids_x, ids_to = slice(5, 10), slice(21, 26)
            sto_x, sto_to = slice(5, 9), slice(21, 25)
        if dy == 0:
            ids_y, sto_y, ids_dst, sto_dst, bc_dst = slice(0, 8), slice(0, 8), ia, sa, ba
        elif dy == 1:
            ids_y, sto_y, ids_dst, sto_dst, bc_dst = slice(3, 8), slice(4, 8), ip, sb, bb
        else:
            ids_y, sto_y, ids_dst, sto_dst, bc_dst = slice(0, 5), slice(0, 4), inn, sb, bb
        place = 1 - dx
        place = {1: 1, 0: 0, 2: 2}[place]
        moves = [
            (sa.at[:, sto_x, sto_y, :], sto_dst.at[:, sto_to, sto_y, :]),
            (ia.at[ids_x, ids_y, :], ids_dst.at[ids_to, ids_y, :]),
            (ba.at[1, sto_y, :], bc_dst.at[place, sto_y, :]),
        ]
        for src, dst in moves:
            n = len(first)
            copy = pltpu.make_async_remote_copy(
                src_ref=src,
                dst_ref=dst,
                send_sem=s1.at[n],
                recv_sem=r1.at[n],
                device_id=device(dx, dy),
                device_id_type=MESH,
            )
            copy.start()
            first.append(copy)

    def table(row):
        line = jnp.broadcast_to(props_ref[row : row + 1, :], (8, 16))
        return jnp.concatenate([line, jnp.zeros((8, 112), jnp.float32)], axis=1)

    tab_p, tab_t, tab_e = jnp.sqrt(table(0)), jnp.sqrt(table(1)), table(2)

    def look(tab, ids):
        return jnp.take_along_axis(tab, ids, axis=1, mode="promise_in_bounds")

    has_n = (gy < n_gy - 1).astype(jnp.float32)
    has_p = (gy > 0).astype(jnp.float32)

    has_w = (gx > 0).astype(jnp.float32)
    has_e = (gx < n_gx - 1).astype(jnp.float32)
    inside_b = jnp.where(rows < 4, has_n, has_p)

    for copy in first:
        copy.wait_recv()

    def gather(p):
        inside = ((p >= OWN) | (gx > 0)) & ((p < OWN + CX) | (gx < n_gx - 1))
        inside = inside.astype(jnp.float32)
        id_a, id_n, id_p = ia[p], inn[p], ip[p]
        for f, tab in enumerate((tab_p, tab_t)):
            ga[f, p] = look(tab, id_a) * inside
            n_tile = look(tab, id_n) * (inside * has_n)
            p_tile = look(tab, id_p) * (inside * has_p)
            gn[f, p] = n_tile
            gp[f, p] = p_tile
            gb[f, p] = jnp.where(rows < 4, n_tile, p_tile)
        ea[p] = look(tab_e, id_a)
        eb[p] = jnp.where(rows < 4, look(tab_e, id_n), look(tab_e, id_p))

    def gather_two(p):
        gather(p)
        gather(p + 1)

    planes(0, EX, 2, gather_two)

    loads[2].wait()

    def inverse(g_p, g_t, e, lap_p, lap_t, sto):
        sp, spt, stp, st = sto
        first_ = sp + lap_p
        last = st + lap_t
        cross = stp + e * lap_p
        det = 1.0 / (first_ * last - cross * spt)
        k11 = g_p * (last - e * spt) * det
        k12 = g_p * (e * sp - stp) * det
        k21 = -(g_t * spt) * det
        k22 = g_t * first_ * det
        return k11, k12, k21, k22

    def coefficients(p, own):
        west = (p < OWN).astype(jnp.int32)
        east = (p >= OWN + CX).astype(jnp.int32)
        place = 1 - west + east
        lane = p - OWN + 16 * west - 16 * east
        shift = 127 - lane
        top = lanes == 127
        bc_a = jnp.where(top, pltpu.roll(ba[place], shift, 1), 0.0)
        bc_b = jnp.where(top, pltpu.roll(bb[place], shift, 1), 0.0)
        laps_a, laps_b = [], []
        for f in range(2):
            a, b, n_tile, p_tile = ga[f, p], gb[f, p], gn[f, p], gp[f, p]
            a_up, a_down = pltpu.roll(a, 7, 0), pltpu.roll(a, 1, 0)
            b_up, b_down = pltpu.roll(b, 7, 0), pltpu.roll(b, 1, 0)
            y_a = jnp.where(rows == 7, b_up, a_up) + jnp.where(rows == 0, b_down, a_down)
            n_up, n_down = pltpu.roll(n_tile, 7, 0), pltpu.roll(n_tile, 1, 0)
            p_up, p_down = pltpu.roll(p_tile, 7, 0), pltpu.roll(p_tile, 1, 0)
            up = jnp.where(rows < 4, n_up, jnp.where(rows == 7, a_up, p_up))
            down = jnp.where(rows < 4, jnp.where(rows == 0, a_down, n_down), p_down)
            y_b = up + down
            laps_a.append(a * (ga[f, p - 1] + ga[f, p + 1] + y_a + z_sum(a, lanes)))
            laps_b.append(b * (gb[f, p - 1] + gb[f, p + 1] + y_b + z_sum(b, lanes)))
        for tile, (laps, bc, g_ref, e_ref, s_ref) in enumerate(
            ((laps_a, bc_a, ga, ea, sa), (laps_b, bc_b, gb, eb, sb))
        ):
            g_p, g_t, e = g_ref[0, p], g_ref[1, p], e_ref[p]
            lap_p = laps[0] + 2.0 * (g_p * g_p) * bc
            lap_t = laps[1]
            sto = [s_ref[i, p] for i in range(4)]
            k11, k12, k21, k22 = inverse(g_p, g_t, e, lap_p, lap_t, sto)
            m[0, tile, p] = k11 * g_p
            m[1, tile, p] = k12 * g_t
            m[2, tile, p] = k21 * g_p
            m[3, tile, p] = k22 * g_t
            if own and tile == 0:
                x = p - OWN
                for i, value in enumerate((k11, k12, k21, k22)):
                    k_own[i, x] = value
                lap[0, x] = lap_p
                lap[1, x] = sto[3] + lap_t
                recip[0, x] = 1.0 / g_p
                recip[1, x] = 1.0 / g_t
                u, t = source[0, x], source[1, x]
                rhs[0, p] = k11 * u + k12 * t
                rhs[1, p] = k21 * u + k22 * t

    planes(1, OWN, 2, lambda p: [coefficients(p + i, False) for i in range(2)])
    planes(OWN, OWN + CX, 2, lambda p: [coefficients(p + i, True) for i in range(2)])
    planes(OWN + CX, EX - 1, 2, lambda p: [coefficients(p + i, False) for i in range(2)])

    def solve():
        def start(p):
            for i in range(6):
                for f in range(2):
                    z[0, f, 0, p + i] = rhs[f, p + i]
                    z[0, f, 1, p + i] = zero

        planes(1, EX - 1, 6, start)

        def sweep(index, carry):
            old = lax.rem(index, 2)
            new = 1 - old

            def update(p):
                count = 6
                win = [
                    [[z[old, f, tile, p + i - 1] for tile in range(2)] for i in range(count + 2)]
                    for f in range(2)
                ]
                for i in range(count):
                    sums = []
                    for f in range(2):
                        left, mid, right = win[f][i], win[f][i + 1], win[f][i + 2]
                        sums.append(ring_sum(left, mid[0], mid[1], right, rows, lanes))
                    for tile in range(2):
                        sum_q, sum_t = sums[0][tile], sums[1][tile]
                        for f in range(2):
                            value = (
                                m[2 * f, tile, p + i] * sum_q + m[2 * f + 1, tile, p + i] * sum_t
                            )
                            if tile == 0:
                                value = value + rhs[f, p + i]
                            z[new, f, tile, p + i] = value

            planes(1, EX - 1, 6, update)
            return carry

        lax.fori_loop(0, SWEEPS - 1, sweep, 0)

    last_slot = (SWEEPS - 1) % 2

    def exchange(turn, ssem, rsem):
        copies = []
        for dx, dy in SIDES:
            side = 0 if dx == 1 else 1
            wide = slice(20, 25) if dx == 1 else slice(1, 6)
            narrow = slice(21, 25) if dx == 1 else slice(1, 5)
            half = slice(0, 4) if dy == 1 else slice(4, 8)
            line = slice(7, 8) if dy == 1 else slice(0, 1)
            if dy == 0:
                moves = [(z.at[last_slot, :, :, wide], rx.at[turn, side])]
            elif dx == 0:
                moves = [
                    (z.at[last_slot, :, 1, 4:22, half, :], rya.at[turn, :, :, half, :]),
                    (z.at[last_slot, :, 0, 5:21, line, :], ryb.at[turn, :, :, line, :]),
                ]
            else:
                moves = [
                    (z.at[last_slot, :, 1, wide, half, :], rca.at[turn, side, :, :, half, :]),
                    (z.at[last_slot, :, 0, narrow, line, :], rcb.at[turn, side, :, :, line, :]),
                ]
            for src, dst in moves:
                n = len(copies)
                copy = pltpu.make_async_remote_copy(
                    src_ref=src,
                    dst_ref=dst,
                    send_sem=ssem.at[turn, n],
                    recv_sem=rsem.at[turn, n],
                    device_id=device(dx, dy),
                    device_id_type=MESH,
                )
                copy.start()
                copies.append(copy)
        return copies

    def add_up(turn):
        def one(p, west, east):
            for f in range(2):
                a = z[last_slot, f, 0, p] + rya[turn, f, p - 4]
                b = z[last_slot, f, 1, p]
                if west:
                    a = a + (rx[turn, 0, f, 0, p - 4] + rca[turn, 0, f, p - 4])
                if east:
                    a = a + (rx[turn, 1, f, 0, p - 17] + rca[turn, 1, f, p - 17])
                if isinstance(p, int) and p == 4:
                    a = a * has_w
                if isinstance(p, int) and p == 21:
                    a = a * has_e
                fold[f, 0, p - 4] = a
                if not isinstance(p, int) or 5 <= p <= 20:
                    b = b + ryb[turn, f, p - 5]
                    if west:
                        b = b + (rx[turn, 0, f, 1, p - 4] + rcb[turn, 0, f, p - 5])
                    if east:
                        b = b + (rx[turn, 1, f, 1, p - 17] + rcb[turn, 1, f, p - 17])
                    fold[f, 1, p - 4] = b * inside_b

        for p in range(4, 9):
            one(p, True, False)
        planes(9, 17, 4, lambda p: [one(p + i, False, False) for i in range(4)])
        for p in range(17, 22):
            one(p, False, True)

    def apply(turn):
        def one(x, acc):
            i = x + 1
            sums, values = [], []
            for f in range(2):
                a, b = fold[f, 0, i], fold[f, 1, i]
                y_up = jnp.where(rows == 7, pltpu.roll(b, 7, 0), pltpu.roll(a, 7, 0))
                y_down = jnp.where(rows == 0, pltpu.roll(b, 1, 0), pltpu.roll(a, 1, 0))
                near = fold[f, 0, i - 1] + fold[f, 0, i + 1]
                sums.append(near + ((y_up + y_down) + z_sum(a, lanes)))
                values.append(a)
            p = x + OWN
            sp, spt, stp, st = [sa[j, p] for j in range(4)]
            q = values[0] * recip[0, x]
            t = values[1] * recip[1, x]
            u = q - ea[p] * t
            keep_p[turn, 0, x] = u
            keep_p[turn, 1, x] = t
            w_p = sp * u + lap[0, x] * q + stp * t - ga[0, p] * sums[0]
            w_t = spt * u + lap[1, x] * t - ga[1, p] * sums[1]
            src_p, src_t = source[0, x], source[1, x]
            if turn == 0:
                d_p, d_t = w_p - src_p, w_t - src_t
                rhs[0, p] = k_own[0, x] * d_p + k_own[1, x] * d_t
                rhs[1, p] = k_own[2, x] * d_p + k_own[3, x] * d_t
                terms = [(src_p, src_t, src_p, src_t), (src_p, src_t, d_p, d_t), (d_p, d_t, d_p, d_t)]
            else:
                o_p, o_t = keep_d[0, 0, x], keep_d[0, 1, x]
                d_p, d_t = w_p - o_p, w_t - o_t
                terms = [(src_p, src_t, d_p, d_t), (o_p, o_t, d_p, d_t), (d_p, d_t, d_p, d_t)]
            keep_d[turn, 0, x] = d_p
            keep_d[turn, 1, x] = d_t
            return tuple(
                total + (one_ * two + three * four)
                for total, (one_, three, two, four) in zip(acc, terms)
            )

        def group(index, acc):
            for i in range(4):
                acc = one(index * 4 + i, acc)
            return acc

        return lax.fori_loop(0, CX // 4, group, (zero, zero, zero))

    solve()
    copies = exchange(0, s2, r2)
    for copy in copies:
        copy.wait_recv()
    add_up(0)
    dots_a = apply(0)
    for copy in copies:
        copy.wait_send()
    solve()
    copies = exchange(1, s2, r2)
    for copy in copies:
        copy.wait_recv()
    add_up(1)
    dots_b = apply(1)

    ordered = [dots_a[0], dots_a[1], dots_b[0], dots_a[2], dots_b[1], dots_b[2]]
    tile = zero
    for i, part in enumerate(ordered):
        tile = jnp.where(rows == i, total_rows(part), tile)

    def all_sum(tile, box, me, size, partner, ssem, rsem):
        box[me] = tile

        def copy_of(step):
            return pltpu.make_async_remote_copy(
                src_ref=box.at[me],
                dst_ref=box.at[me],
                send_sem=ssem.at[step],
                recv_sem=rsem.at[step],
                device_id=partner(step),
                device_id_type=MESH,
            )

        def send(step, carry):
            copy_of(step).start()
            return carry

        def receive(step, carry):
            copy_of(step).wait_recv()
            return carry

        lax.fori_loop(1, size, send, 0)
        lax.fori_loop(1, size, receive, 0)
        parts = [box[i] for i in range(size)]
        while len(parts) > 1:
            parts = [parts[i] + parts[i + 1] for i in range(0, len(parts), 2)]
        return parts[0], copy_of

    tile, copy1 = all_sum(tile, g1, me1, size1, partner1, s3, r3)
    tile, copy2 = all_sum(tile, g2, me2, size2, partner2, s4, r4)
    factors = small_problem(total_lanes(tile))
    a1, a2, q1, q2, q3, v1, v2, v3 = [jnp.broadcast_to(f, (8, 128)) for f in factors]
    v1, v2, v3 = v1 * scale, v2 * scale, v3 * scale

    def combine(x):
        for i in range(2):
            for f in range(2):
                s, d1, d2 = source[f, x + i], keep_d[0, f, x + i], keep_d[1, f, x + i]
                adjoint_ref[f, x + i] = a1 * keep_p[0, f, x + i] + a2 * keep_p[1, f, x + i]
                residual_ref[f, x + i] = q1 * s + q2 * d1 + q3 * d2
                next_ref[f, x + i] = v1 * s + v2 * d1 + v3 * d2

    planes(0, CX, 2, combine)

    def drain1(step, carry):
        copy1(step).wait_send()
        return carry

    def drain2(step, carry):
        copy2(step).wait_send()
        return carry

    for copy in first:
        copy.wait_send()
    for copy in copies:
        copy.wait_send()
    lax.fori_loop(1, size1, drain1, 0)
    lax.fori_loop(1, size2, drain2, 0)


def shards(adjoint_source, storage, soil_ids, bc_mask, soil_props):
    f32 = jnp.float32
    cells = 2.0 * 16 * lax.axis_size("gx") * 8 * lax.axis_size("gy") * 128
    out = jax.ShapeDtypeStruct(adjoint_source.shape, f32)
    any_spec = pl.BlockSpec(memory_space=pl.ANY)
    vmem = pl.BlockSpec(memory_space=pltpu.VMEM)

    def buf(*lead, dtype=f32):
        return pltpu.VMEM(tuple(lead) + (8, 128), dtype)

    i32 = jnp.int32
    dma = pltpu.SemaphoreType.DMA
    return pl.pallas_call(
        functools.partial(kernel, math.sqrt(cells)),
        out_shape=(out, out, out),
        in_specs=[any_spec, any_spec, any_spec, vmem, vmem],
        out_specs=(vmem, vmem, vmem),
        scratch_shapes=[
            buf(2, CX),
            buf(4, EX), buf(4, EX),
            buf(EX, dtype=i32), buf(EX, dtype=i32), buf(EX, dtype=i32),
            buf(3), buf(3),
            buf(2, EX), buf(2, EX), buf(2, EX), buf(2, EX),
            buf(EX), buf(EX),
            buf(4, 2, EX),
            buf(4, CX), buf(2, CX), buf(2, CX),
            buf(2, EX),
            buf(2, 2, 2, EX),
            buf(2, 2, 18),
            buf(2, 2, CX), buf(2, 2, CX),
            buf(2, 2, 18), buf(2, 2, 16),
            buf(2, 2, 2, 2, 5),
            buf(2, 2, 2, 5), buf(2, 2, 2, 4),
            buf(16), buf(16),
            dma((3,)),
            dma((24,)), dma((24,)),
            dma((2, 14)), dma((2, 14)),
            dma((16,)), dma((16,)),
            dma((16,)), dma((16,)),
        ],
        compiler_params=pltpu.CompilerParams(
            collective_id=0, has_side_effects=True, vmem_limit_bytes=24 << 20
        ),
    )(adjoint_source, storage, soil_ids, bc_mask.T, soil_props)


def solution(mesh):
    in_specs = (
        P(None, "gx", "gy", None),
        P(None, "gx", "gy", None),
        P("gx", "gy", None),
        P("gx", "gy"),
        P(),
    )
    out_specs = (P(None, "gx", "gy", None), P(None, "gx", "gy", None), P(None, "gx", "gy", None))
    return jax.shard_map(shards, mesh=mesh, in_specs=in_specs, out_specs=out_specs, check_vma=False)
```

```python
import functools
import math

import jax
import jax.numpy as jnp
from jax import lax
from jax.experimental import pallas as pl
from jax.experimental.pallas import tpu as pltpu
from jax.sharding import PartitionSpec as P

MESH = pl.DeviceIdType.MESH
CX = 16
EX = 26
OWN = 5
SWEEPS = 6
epsilon = 1e-06


SIDES = [(dx, dy) for dy in (1, -1, 0) for dx in (0, 1, -1) if (dx, dy) != (0, 0)]


def planes(low, high, chunk, body):
    count = (high - low) // chunk

    def group(index, carry):
        body(low + index * chunk)
        return carry

    lax.fori_loop(0, count, group, 0)


def ring_sum(left, a, b, right, rows, lanes):
    a_up, b_up = pltpu.roll(a, 7, 0), pltpu.roll(b, 7, 0)
    a_down, b_down = pltpu.roll(a, 1, 0), pltpu.roll(b, 1, 0)
    y_a = jnp.where(rows == 7, b_up, a_up) + jnp.where(rows == 0, b_down, a_down)
    b_high = jnp.where(rows == 7, a_up, jnp.where(rows == 3, 0.0, b_up))
    b_low = jnp.where(rows == 0, a_down, jnp.where(rows == 4, 0.0, b_down))
    y_b = b_high + b_low
    out_a = (left[0] + right[0]) + (y_a + z_sum(a, lanes))
    out_b = (left[1] + right[1]) + (y_b + z_sum(b, lanes))
    return out_a, out_b


def z_sum(tile, lanes):
    below = jnp.where(lanes == 0, 0.0, pltpu.roll(tile, 1, 1))
    above = jnp.where(lanes == 127, 0.0, pltpu.roll(tile, 127, 1))
    return below + above


def total_rows(tile):
    tile = tile + pltpu.roll(tile, 4, 0)
    tile = tile + pltpu.roll(tile, 2, 0)
    return tile + pltpu.roll(tile, 1, 0)


def total_lanes(tile):
    for shift in (64, 32, 16, 8, 4, 2, 1):
        tile = tile + pltpu.roll(tile, shift, 1)
    return tile


def small_problem(gram, size):
    ss, s1, s2, d11, d12, d22 = [gram[i : i + 1] for i in range(6)]
    square = ss + epsilon
    beta = jnp.sqrt(square)
    g1 = (epsilon - s1) / square
    h11 = 1.0 - g1
    norm1 = (d11 + 2.0 * g1 * s1 + g1 * g1 * ss) / square
    h21 = jnp.sqrt(jnp.maximum(norm1, 0.0) + epsilon)
    al = 1.0 / (beta * h21)
    ga = g1 * al
    h12 = (al * (s1 + s2) + ga * (ss + s1)) / beta
    v22 = al * al * d11 + 2.0 * al * ga * s1 + ga * ga * ss
    e22 = al * (al * d12 + ga * d11) + ga * (al * s2 + ga * s1)
    h22 = v22 + e22
    x3 = al
    x2 = ga + (1.0 - h22) * al
    x1 = (1.0 - h22) * ga - h12 / beta
    norm2 = (
        x3 * x3 * d22
        + x2 * x2 * d11
        + x1 * x1 * ss
        + 2.0 * (x3 * x2 * d12 + x3 * x1 * s2 + x2 * x1 * s1)
    )
    h32 = jnp.sqrt(jnp.maximum(norm2, 0.0) + epsilon)
    r1 = jnp.sqrt(h11 * h11 + h21 * h21)
    c1, n1 = h11 / r1, h21 / r1
    t0, t1 = c1 * beta, -n1 * beta
    u12 = c1 * h12 + n1 * h22
    low = c1 * h22 - n1 * h12
    r2 = jnp.sqrt(low * low + h32 * h32)
    c2 = low / r2
    y2 = c2 * t1 / r2
    y1 = (t0 - u12 * y2) / r1
    f1 = beta - h11 * y1 - h12 * y2
    f2 = -h21 * y1 - h22 * y2
    f3 = -h32 * y2
    a1, a2 = y1 / beta + y2 * ga, y2 * al
    inv = 1.0 / h32
    v31, v32, v33 = x1 * inv, x2 * inv, x3 * inv
    q1 = f1 / beta + f2 * ga + f3 * v31
    q2 = f2 * al + f3 * v32
    q3 = f3 * v33
    return a1, a2, q1, q2, q3, v31 * size, v32 * size, v33 * size


def kernel(
    scale,
    source_hbm, storage_hbm, ids_hbm, bc_hbm, props_hbm,
    p1_hbm, p2_hbm, d1_hbm, d2_hbm, factors_ref,
    bc_ref, props_ref, source, sa, sb, ia, inn, ip, ba, bb,
    ga, gb, gn, gp, ea, eb, m, k_own, lap, recip, rhs, z, fold, keep_p, keep_d,
    rya, ryb, rx, rca, rcb, g1, g2,
    local_sem, s1, r1, s2, r2, s3, r3, s4, r4,
):
    gx, gy = lax.axis_index("gx"), lax.axis_index("gy")
    n_gx, n_gy = lax.axis_size("gx"), lax.axis_size("gy")
    rows = lax.broadcasted_iota(jnp.int32, (8, 128), 0)
    lanes = lax.broadcasted_iota(jnp.int32, (8, 128), 1)
    zero = jnp.zeros((8, 128), jnp.float32)

    def device(dx, dy):
        x = lax.rem(gx + (dx + n_gx), n_gx) if dx else gx
        y = lax.rem(gy + (dy + n_gy), n_gy) if dy else gy
        return x, y

    loads = [
        pltpu.make_async_copy(storage_hbm, sa.at[:, OWN : OWN + CX], local_sem.at[0]),
        pltpu.make_async_copy(ids_hbm, ia.at[OWN : OWN + CX], local_sem.at[1]),
        pltpu.make_async_copy(source_hbm, source, local_sem.at[2]),
        pltpu.make_async_copy(bc_hbm, bc_ref, local_sem.at[3]),
        pltpu.make_async_copy(props_hbm, props_ref, local_sem.at[4]),
    ]
    for copy in loads:
        copy.start()

    size1, size2 = n_gx * 4, n_gy // 4
    me1 = gx * 4 + lax.rem(gy, 4)
    me2 = lax.div(gy, 4)

    def partner1(step):
        other = lax.rem(me1 + step, size1)
        return lax.div(other, 4), me2 * 4 + lax.rem(other, 4)

    def partner2(step):
        other = lax.rem(me2 + step, size2)
        return gx, other * 4 + lax.rem(gy, 4)

    barrier = pltpu.get_barrier_semaphore()
    for dx, dy in SIDES:
        pl.semaphore_signal(barrier, inc=1, device_id=device(dx, dy), device_id_type=MESH)

    def greet(step, carry):
        pl.semaphore_signal(barrier, inc=1, device_id=partner1(step), device_id_type=MESH)
        return carry

    def greet2(step, carry):
        pl.semaphore_signal(barrier, inc=1, device_id=partner2(step), device_id_type=MESH)
        return carry

    lax.fori_loop(1, size1, greet, 0)
    lax.fori_loop(1, size2, greet2, 0)

    loads[3].wait()
    own_bc = jnp.concatenate(
        [bc_ref[...].astype(jnp.float32), jnp.zeros((8, 112), jnp.float32)], axis=1
    )
    ba[1] = own_bc
    for slot in range(2):
        for field in range(2):
            for tile in range(2):
                z[slot, field, tile, 0] = zero
                z[slot, field, tile, EX - 1] = zero
    for field in range(2):
        for p in list(range(0, OWN)) + list(range(OWN + CX, EX)):
            rhs[field, p] = zero

    pl.semaphore_wait(barrier, len(SIDES) + size1 - 1 + size2 - 1)
    loads[1].wait()

    first = []

    def push(src, dst, dx, dy):
        n = len(first)
        copy = pltpu.make_async_remote_copy(
            src_ref=src,
            dst_ref=dst,
            send_sem=s1.at[n],
            recv_sem=r1.at[n],
            device_id=device(dx, dy),
            device_id_type=MESH,
        )
        copy.start()
        first.append(copy)

    for dx, dy in SIDES:
        src_x = {0: slice(5, 21), 1: slice(16, 21), -1: slice(5, 10)}[dx]
        dst_x = {0: slice(5, 21), 1: slice(0, 5), -1: slice(21, 26)}[dx]
        y = {0: slice(0, 8), 1: slice(3, 8), -1: slice(0, 5)}[dy]
        half = {0: slice(0, 8), 1: slice(4, 8), -1: slice(0, 4)}[dy]
        place = {0: 1, 1: 0, -1: 2}[dx]
        push(ia.at[src_x, y, :], {0: ia, 1: ip, -1: inn}[dy].at[dst_x, y, :], dx, dy)
        push(ba.at[1, half, :], (bb if dy else ba).at[place, half, :], dx, dy)
    n_ids = len(first)
    loads[0].wait()
    for dx, dy in SIDES:
        src_x = {0: slice(5, 21), 1: slice(17, 21), -1: slice(5, 9)}[dx]
        dst_x = {0: slice(5, 21), 1: slice(1, 5), -1: slice(21, 25)}[dx]
        half = {0: slice(0, 8), 1: slice(4, 8), -1: slice(0, 4)}[dy]
        push(sa.at[:, src_x, half, :], (sb if dy else sa).at[:, dst_x, half, :], dx, dy)

    loads[4].wait()

    def table(row):
        line = jnp.broadcast_to(props_ref[row : row + 1, :], (8, 16))
        return jnp.concatenate([line, jnp.zeros((8, 112), jnp.float32)], axis=1)

    tab_p, tab_t, tab_e = jnp.sqrt(table(0)), jnp.sqrt(table(1)), table(2)

    def look(tab, ids):
        return jnp.take_along_axis(tab, ids, axis=1, mode="promise_in_bounds")

    has_n = (gy < n_gy - 1).astype(jnp.float32)
    has_p = (gy > 0).astype(jnp.float32)

    has_w = (gx > 0).astype(jnp.float32)
    has_e = (gx < n_gx - 1).astype(jnp.float32)
    inside_b = jnp.where(rows < 4, has_n, has_p)

    for copy in first[:n_ids]:
        copy.wait_recv()

    def gather(p):
        inside = ((p >= OWN) | (gx > 0)) & ((p < OWN + CX) | (gx < n_gx - 1))
        inside = inside.astype(jnp.float32)
        id_a, id_n, id_p = ia[p], inn[p], ip[p]
        for f, tab in enumerate((tab_p, tab_t)):
            ga[f, p] = look(tab, id_a) * inside
            n_tile = look(tab, id_n) * (inside * has_n)
            p_tile = look(tab, id_p) * (inside * has_p)
            gn[f, p] = n_tile
            gp[f, p] = p_tile
            gb[f, p] = jnp.where(rows < 4, n_tile, p_tile)
        ea[p] = look(tab_e, id_a)
        eb[p] = jnp.where(rows < 4, look(tab_e, id_n), look(tab_e, id_p))

    def gather_two(p):
        gather(p)
        gather(p + 1)

    planes(0, EX, 2, gather_two)

    loads[2].wait()

    def inverse(g_p, g_t, e, lap_p, lap_t, sto):
        sp, spt, stp, st = sto
        first_ = sp + lap_p
        last = st + lap_t
        cross = stp + e * lap_p
        det = 1.0 / (first_ * last - cross * spt)
        k11 = g_p * (last - e * spt) * det
        k12 = g_p * (e * sp - stp) * det
        k21 = -(g_t * spt) * det
        k22 = g_t * first_ * det
        return k11, k12, k21, k22

    def diagonals(p):
        west = (p < OWN).astype(jnp.int32)
        east = (p >= OWN + CX).astype(jnp.int32)
        place = 1 - west + east
        shift = 127 - (p - OWN + 16 * west - 16 * east)
        top = lanes == 127
        bounds = [jnp.where(top, pltpu.roll(ref[place], shift, 1), 0.0) for ref in (ba, bb)]
        for f in range(2):
            a, b, n_tile, p_tile = ga[f, p], gb[f, p], gn[f, p], gp[f, p]
            a_up, a_down = pltpu.roll(a, 7, 0), pltpu.roll(a, 1, 0)
            b_up, b_down = pltpu.roll(b, 7, 0), pltpu.roll(b, 1, 0)
            y_a = jnp.where(rows == 7, b_up, a_up) + jnp.where(rows == 0, b_down, a_down)
            n_up, n_down = pltpu.roll(n_tile, 7, 0), pltpu.roll(n_tile, 1, 0)
            p_up, p_down = pltpu.roll(p_tile, 7, 0), pltpu.roll(p_tile, 1, 0)
            up = jnp.where(rows < 4, n_up, jnp.where(rows == 7, a_up, p_up))
            down = jnp.where(rows < 4, jnp.where(rows == 0, a_down, n_down), p_down)
            y_b = up + down
            lap_a = a * (ga[f, p - 1] + ga[f, p + 1] + y_a + z_sum(a, lanes))
            lap_b = b * (gb[f, p - 1] + gb[f, p + 1] + y_b + z_sum(b, lanes))
            if f == 0:
                lap_a = lap_a + 2.0 * (a * a) * bounds[0]
                lap_b = lap_b + 2.0 * (b * b) * bounds[1]
            lap[f, 0, p] = lap_a
            lap[f, 1, p] = lap_b

    def invert(p, tile, own):
        g_ref, e_ref, s_ref = ((ga, ea, sa), (gb, eb, sb))[tile]
        g_p, g_t, e = g_ref[0, p], g_ref[1, p], e_ref[p]
        sto = [s_ref[i, p] for i in range(4)]
        k11, k12, k21, k22 = inverse(g_p, g_t, e, lap[0, tile, p], lap[1, tile, p], sto)
        m[0, tile, p] = k11 * g_p
        m[1, tile, p] = k12 * g_t
        m[2, tile, p] = k21 * g_p
        m[3, tile, p] = k22 * g_t
        if own:
            x = p - OWN
            for i, value in enumerate((k11, k12, k21, k22)):
                k_own[i, x] = value
            recip[0, x] = 1.0 / g_p
            recip[1, x] = 1.0 / g_t
            u, t = source[0, x], source[1, x]
            rhs[0, p] = k11 * u + k12 * t
            rhs[1, p] = k21 * u + k22 * t

    planes(1, EX - 1, 2, lambda p: [diagonals(p + i) for i in range(2)])
    planes(OWN, OWN + CX, 4, lambda p: [invert(p + i, 0, True) for i in range(4)])
    for copy in first[n_ids:]:
        copy.wait_recv()
    planes(1, EX - 1, 4, lambda p: [invert(p + i, 1, False) for i in range(4)])
    planes(1, OWN, 4, lambda p: [invert(p + i, 0, False) for i in range(4)])
    planes(OWN + CX, EX - 1, 4, lambda p: [invert(p + i, 0, False) for i in range(4)])

    def solve():
        def start(p):
            for i in range(6):
                for f in range(2):
                    z[0, f, 0, p + i] = rhs[f, p + i]
                    z[0, f, 1, p + i] = zero

        planes(1, EX - 1, 6, start)

        def sweep(index, carry):
            old = lax.rem(index, 2)
            new = 1 - old

            def update(p):
                count = 6
                win = [
                    [[z[old, f, tile, p + i - 1] for tile in range(2)] for i in range(count + 2)]
                    for f in range(2)
                ]
                for i in range(count):
                    sums = []
                    for f in range(2):
                        left, mid, right = win[f][i], win[f][i + 1], win[f][i + 2]
                        sums.append(ring_sum(left, mid[0], mid[1], right, rows, lanes))
                    for tile in range(2):
                        sum_q, sum_t = sums[0][tile], sums[1][tile]
                        for f in range(2):
                            value = (
                                m[2 * f, tile, p + i] * sum_q + m[2 * f + 1, tile, p + i] * sum_t
                            )
                            if tile == 0:
                                value = value + rhs[f, p + i]
                            z[new, f, tile, p + i] = value

            planes(1, EX - 1, 6, update)
            return carry

        lax.fori_loop(0, SWEEPS - 1, sweep, 0)

    last_slot = (SWEEPS - 1) % 2

    def exchange(turn, ssem, rsem):
        copies = []
        for dx, dy in SIDES:
            side = 0 if dx == 1 else 1
            wide = slice(20, 25) if dx == 1 else slice(1, 6)
            narrow = slice(21, 25) if dx == 1 else slice(1, 5)
            narrow_to = slice(1, 5) if dx == 1 else slice(0, 4)
            half = slice(0, 4) if dy == 1 else slice(4, 8)
            line = slice(7, 8) if dy == 1 else slice(0, 1)
            if dy == 0:
                moves = [(z.at[last_slot, :, 0, wide], rx.at[turn, side, :, 0])]
                for edge in (slice(0, 1), slice(7, 8)):
                    moves.append(
                        (
                            z.at[last_slot, :, 1, narrow, edge, :],
                            rx.at[turn, side, :, 1, narrow_to, edge, :],
                        )
                    )
            elif dx == 0:
                moves = [
                    (z.at[last_slot, :, 1, 4:22, half, :], rya.at[turn, :, :, half, :]),
                    (z.at[last_slot, :, 0, 5:21, line, :], ryb.at[turn, :, :, line, :]),
                ]
            else:
                moves = [
                    (z.at[last_slot, :, 1, wide, half, :], rca.at[turn, side, :, :, half, :]),
                    (z.at[last_slot, :, 0, narrow, line, :], rcb.at[turn, side, :, :, line, :]),
                ]
            for src, dst in moves:
                n = len(copies)
                copy = pltpu.make_async_remote_copy(
                    src_ref=src,
                    dst_ref=dst,
                    send_sem=ssem.at[turn, n],
                    recv_sem=rsem.at[turn, n],
                    device_id=device(dx, dy),
                    device_id_type=MESH,
                )
                copy.start()
                copies.append(copy)
        return copies

    def add_up(turn):
        def one(p, west, east):
            for f in range(2):
                a = z[last_slot, f, 0, p] + rya[turn, f, p - 4]
                b = z[last_slot, f, 1, p]
                if west:
                    a = a + (rx[turn, 0, f, 0, p - 4] + rca[turn, 0, f, p - 4])
                if east:
                    a = a + (rx[turn, 1, f, 0, p - 17] + rca[turn, 1, f, p - 17])
                if isinstance(p, int) and p == 4:
                    a = a * has_w
                if isinstance(p, int) and p == 21:
                    a = a * has_e
                fold[f, 0, p - 4] = a
                if not isinstance(p, int) or 5 <= p <= 20:
                    b = b + ryb[turn, f, p - 5]
                    if west:
                        b = b + (rx[turn, 0, f, 1, p - 4] + rcb[turn, 0, f, p - 5])
                    if east:
                        b = b + (rx[turn, 1, f, 1, p - 17] + rcb[turn, 1, f, p - 17])
                    fold[f, 1, p - 4] = b * inside_b

        for p in range(4, 9):
            one(p, True, False)
        planes(9, 17, 4, lambda p: [one(p + i, False, False) for i in range(4)])
        for p in range(17, 22):
            one(p, False, True)

    def apply(turn):
        def one(x, acc):
            i = x + 1
            sums, values = [], []
            for f in range(2):
                a, b = fold[f, 0, i], fold[f, 1, i]
                y_up = jnp.where(rows == 7, pltpu.roll(b, 7, 0), pltpu.roll(a, 7, 0))
                y_down = jnp.where(rows == 0, pltpu.roll(b, 1, 0), pltpu.roll(a, 1, 0))
                near = fold[f, 0, i - 1] + fold[f, 0, i + 1]
                sums.append(near + ((y_up + y_down) + z_sum(a, lanes)))
                values.append(a)
            p = x + OWN
            sp, spt, stp, st = [sa[j, p] for j in range(4)]
            q = values[0] * recip[0, x]
            t = values[1] * recip[1, x]
            u = q - ea[p] * t
            keep_p[turn, 0, x] = u
            keep_p[turn, 1, x] = t
            w_p = sp * u + lap[0, 0, p] * q + stp * t - ga[0, p] * sums[0]
            w_t = spt * u + (st + lap[1, 0, p]) * t - ga[1, p] * sums[1]
            src_p, src_t = source[0, x], source[1, x]
            if turn == 0:
                d_p, d_t = w_p - src_p, w_t - src_t
                rhs[0, p] = k_own[0, x] * d_p + k_own[1, x] * d_t
                rhs[1, p] = k_own[2, x] * d_p + k_own[3, x] * d_t
                terms = [(src_p, src_t, src_p, src_t), (src_p, src_t, d_p, d_t), (d_p, d_t, d_p, d_t)]
            else:
                o_p, o_t = keep_d[0, 0, x], keep_d[0, 1, x]
                d_p, d_t = w_p - o_p, w_t - o_t
                terms = [(src_p, src_t, d_p, d_t), (o_p, o_t, d_p, d_t), (d_p, d_t, d_p, d_t)]
            keep_d[turn, 0, x] = d_p
            keep_d[turn, 1, x] = d_t
            return tuple(
                total + (one_ * two + three * four)
                for total, (one_, three, two, four) in zip(acc, terms)
            )

        def group(index, acc):
            for i in range(4):
                acc = one(index * 4 + i, acc)
            return acc

        return lax.fori_loop(0, CX // 4, group, (zero, zero, zero))

    def store(src, dst, n):
        copy = pltpu.make_async_copy(src, dst, local_sem.at[n])
        copy.start()
        return copy

    solve()
    copies = exchange(0, s2, r2)
    for copy in copies:
        copy.wait_recv()
    add_up(0)
    dots_a = apply(0)
    stores = [store(keep_p.at[0], p1_hbm, 5), store(keep_d.at[0], d1_hbm, 6)]
    for copy in copies:
        copy.wait_send()
    solve()
    copies = exchange(1, s2, r2)
    for copy in copies:
        copy.wait_recv()
    add_up(1)
    dots_b = apply(1)
    stores += [store(keep_p.at[1], p2_hbm, 7), store(keep_d.at[1], d2_hbm, 8)]

    ordered = [dots_a[0], dots_a[1], dots_b[0], dots_a[2], dots_b[1], dots_b[2]]
    tile = zero
    for i, part in enumerate(ordered):
        tile = jnp.where(rows == i, total_rows(part), tile)
    tile = total_rows(jnp.where(rows == lanes, total_lanes(tile), 0.0))[0:1]

    def all_sum(tile, box, me, size, partner, ssem, rsem):
        box[me] = tile

        def copy_of(step):
            return pltpu.make_async_remote_copy(
                src_ref=box.at[me],
                dst_ref=box.at[me],
                send_sem=ssem.at[step],
                recv_sem=rsem.at[step],
                device_id=partner(step),
                device_id_type=MESH,
            )

        def send(step, carry):
            copy_of(step).start()
            return carry

        def receive(step, carry):
            copy_of(step).wait_recv()
            return carry

        lax.fori_loop(1, size, send, 0)
        lax.fori_loop(1, size, receive, 0)
        parts = [box[i] for i in range(size)]
        while len(parts) > 1:
            parts = [parts[i] + parts[i + 1] for i in range(0, len(parts), 2)]
        return parts[0], copy_of

    tile, copy1 = all_sum(tile, g1, me1, size1, partner1, s3, r3)
    tile, copy2 = all_sum(tile, g2, me2, size2, partner2, s4, r4)
    factors = small_problem(total_lanes(jnp.where(rows == lanes, tile, 0.0)), scale)
    table_out = zero
    for i, factor in enumerate(factors):
        table_out = jnp.where(rows == i, factor, table_out)
    factors_ref[...] = table_out

    def drain1(step, carry):
        copy1(step).wait_send()
        return carry

    def drain2(step, carry):
        copy2(step).wait_send()
        return carry

    for copy in stores:
        copy.wait()
    for copy in first:
        copy.wait_send()
    for copy in copies:
        copy.wait_send()
    lax.fori_loop(1, size1, drain1, 0)
    lax.fori_loop(1, size2, drain2, 0)


def shards(adjoint_source, storage, soil_ids, bc_mask, soil_props):
    f32 = jnp.float32
    cells = 2.0 * 16 * lax.axis_size("gx") * 8 * lax.axis_size("gy") * 128
    out = jax.ShapeDtypeStruct(adjoint_source.shape, f32)
    any_spec = pl.BlockSpec(memory_space=pltpu.HBM)
    vmem = pl.BlockSpec(memory_space=pltpu.VMEM)

    def buf(*lead, dtype=f32):
        return pltpu.VMEM(tuple(lead) + (8, 128), dtype)

    i32 = jnp.int32
    dma = pltpu.SemaphoreType.DMA
    p1, p2, d1, d2, factors = pl.pallas_call(
        functools.partial(kernel, math.sqrt(cells)),
        out_shape=(out, out, out, out, jax.ShapeDtypeStruct((8, 128), f32)),
        in_specs=[any_spec] * 5,
        out_specs=(any_spec,) * 4 + (vmem,),
        scratch_shapes=[
            pltpu.VMEM((8, CX), i32), pltpu.VMEM((3, 16), f32),
            buf(2, CX),
            buf(4, EX), buf(4, EX),
            buf(EX, dtype=i32), buf(EX, dtype=i32), buf(EX, dtype=i32),
            buf(3), buf(3),
            buf(2, EX), buf(2, EX), buf(2, EX), buf(2, EX),
            buf(EX), buf(EX),
            buf(4, 2, EX),
            buf(4, CX), buf(2, 2, EX), buf(2, CX),
            buf(2, EX),
            buf(2, 2, 2, EX),
            buf(2, 2, 18),
            buf(2, 2, CX), buf(2, 2, CX),
            buf(2, 2, 18), buf(2, 2, 16),
            buf(2, 2, 2, 2, 5),
            buf(2, 2, 2, 5), buf(2, 2, 2, 4),
            pltpu.VMEM((32, 1, 128), f32), pltpu.VMEM((8, 1, 128), f32),
            dma((9,)),
            dma((24,)), dma((24,)),
            dma((2, 18)), dma((2, 18)),
            dma((32,)), dma((32,)),
            dma((8,)), dma((8,)),
        ],
        compiler_params=pltpu.CompilerParams(
            collective_id=0, has_side_effects=True, vmem_limit_bytes=60 << 20
        ),
    )(adjoint_source, storage, soil_ids, bc_mask.T, soil_props)
    c = [factors[i] for i in range(8)]
    adjoint = c[0] * p1 + c[1] * p2
    residual = c[2] * adjoint_source + c[3] * d1 + c[4] * d2
    next_basis = c[5] * adjoint_source + c[6] * d1 + c[7] * d2
    return adjoint, residual, next_basis


def solution(mesh):
    in_specs = (
        P(None, "gx", "gy", None),
        P(None, "gx", "gy", None),
        P("gx", "gy", None),
        P("gx", "gy"),
        P(),
    )
    out_specs = (P(None, "gx", "gy", None), P(None, "gx", "gy", None), P(None, "gx", "gy", None))
    return jax.shard_map(shards, mesh=mesh, in_specs=in_specs, out_specs=out_specs, check_vma=False)
```

```python
import functools
import math

import jax
import jax.numpy as jnp
from jax import lax
from jax.experimental import pallas as pl
from jax.experimental.pallas import tpu as pltpu
from jax.sharding import PartitionSpec as P

MESH = pl.DeviceIdType.MESH
CX = 16
EX = 26
OWN = 5
SWEEPS = 6
epsilon = 1e-06


SIDES = [(dx, dy) for dy in (1, -1, 0) for dx in (0, 1, -1) if (dx, dy) != (0, 0)]


def planes(low, high, chunk, body):
    count = (high - low) // chunk

    def group(index, carry):
        body(low + index * chunk)
        return carry

    lax.fori_loop(0, count, group, 0)


def ring_sum(left, a, b, right, rows, lanes):
    a_up, b_up = pltpu.roll(a, 7, 0), pltpu.roll(b, 7, 0)
    a_down, b_down = pltpu.roll(a, 1, 0), pltpu.roll(b, 1, 0)
    y_a = jnp.where(rows == 7, b_up, a_up) + jnp.where(rows == 0, b_down, a_down)
    b_high = jnp.where(rows == 7, a_up, jnp.where(rows == 3, 0.0, b_up))
    b_low = jnp.where(rows == 0, a_down, jnp.where(rows == 4, 0.0, b_down))
    y_b = b_high + b_low
    out_a = (left[0] + right[0]) + (y_a + z_sum(a, lanes))
    out_b = (left[1] + right[1]) + (y_b + z_sum(b, lanes))
    return out_a, out_b


def z_sum(tile, lanes):
    below = jnp.where(lanes == 0, 0.0, pltpu.roll(tile, 1, 1))
    above = jnp.where(lanes == 127, 0.0, pltpu.roll(tile, 127, 1))
    return below + above


def total_rows(tile):
    tile = tile + pltpu.roll(tile, 4, 0)
    tile = tile + pltpu.roll(tile, 2, 0)
    return tile + pltpu.roll(tile, 1, 0)


def total_lanes(tile):
    for shift in (64, 32, 16, 8, 4, 2, 1):
        tile = tile + pltpu.roll(tile, shift, 1)
    return tile


def small_problem(gram, size):
    ss, s1, s2, d11, d12, d22 = [gram[i : i + 1] for i in range(6)]
    square = ss + epsilon
    beta = jnp.sqrt(square)
    g1 = (epsilon - s1) / square
    h11 = 1.0 - g1
    norm1 = (d11 + 2.0 * g1 * s1 + g1 * g1 * ss) / square
    h21 = jnp.sqrt(jnp.maximum(norm1, 0.0) + epsilon)
    al = 1.0 / (beta * h21)
    ga = g1 * al
    h12 = (al * (s1 + s2) + ga * (ss + s1)) / beta
    v22 = al * al * d11 + 2.0 * al * ga * s1 + ga * ga * ss
    e22 = al * (al * d12 + ga * d11) + ga * (al * s2 + ga * s1)
    h22 = v22 + e22
    x3 = al
    x2 = ga + (1.0 - h22) * al
    x1 = (1.0 - h22) * ga - h12 / beta
    norm2 = (
        x3 * x3 * d22
        + x2 * x2 * d11
        + x1 * x1 * ss
        + 2.0 * (x3 * x2 * d12 + x3 * x1 * s2 + x2 * x1 * s1)
    )
    h32 = jnp.sqrt(jnp.maximum(norm2, 0.0) + epsilon)
    r1 = jnp.sqrt(h11 * h11 + h21 * h21)
    c1, n1 = h11 / r1, h21 / r1
    t0, t1 = c1 * beta, -n1 * beta
    u12 = c1 * h12 + n1 * h22
    low = c1 * h22 - n1 * h12
    r2 = jnp.sqrt(low * low + h32 * h32)
    c2 = low / r2
    y2 = c2 * t1 / r2
    y1 = (t0 - u12 * y2) / r1
    f1 = beta - h11 * y1 - h12 * y2
    f2 = -h21 * y1 - h22 * y2
    f3 = -h32 * y2
    a1, a2 = y1 / beta + y2 * ga, y2 * al
    inv = 1.0 / h32
    v31, v32, v33 = x1 * inv, x2 * inv, x3 * inv
    q1 = f1 / beta + f2 * ga + f3 * v31
    q2 = f2 * al + f3 * v32
    q3 = f3 * v33
    return a1, a2, q1, q2, q3, v31 * size, v32 * size, v33 * size


def kernel(
    scale,
    source_hbm, storage_hbm, ids_hbm, bc_hbm, props_hbm,
    p1, p2, d1, d2, factors_ref,
    bc_ref, props_ref, source, sa, sb, ia, inn, ip, ba, bb,
    ga, gb, gn, gp, ea, eb, m, k_own, lap, recip, rhs, z, fold,
    rya, ryb, rx, rca, rcb, g1, g2,
    local_sem, s1, r1, s2, r2, s3, r3, s4, r4,
):
    gx, gy = lax.axis_index("gx"), lax.axis_index("gy")
    n_gx, n_gy = lax.axis_size("gx"), lax.axis_size("gy")
    rows = lax.broadcasted_iota(jnp.int32, (8, 128), 0)
    lanes = lax.broadcasted_iota(jnp.int32, (8, 128), 1)
    zero = jnp.zeros((8, 128), jnp.float32)
    keep_p, keep_d = (p1, p2), (d1, d2)

    def device(dx, dy):
        x = lax.rem(gx + (dx + n_gx), n_gx) if dx else gx
        y = lax.rem(gy + (dy + n_gy), n_gy) if dy else gy
        return x, y

    loads = [
        pltpu.make_async_copy(storage_hbm, sa.at[:, OWN : OWN + CX], local_sem.at[0]),
        pltpu.make_async_copy(ids_hbm, ia.at[OWN : OWN + CX], local_sem.at[1]),
        pltpu.make_async_copy(source_hbm, source, local_sem.at[2]),
        pltpu.make_async_copy(bc_hbm, bc_ref, local_sem.at[3]),
        pltpu.make_async_copy(props_hbm, props_ref, local_sem.at[4]),
    ]
    for copy in loads:
        copy.start()

    size1, size2 = n_gx * 4, n_gy // 4
    me1 = gx * 4 + lax.rem(gy, 4)
    me2 = lax.div(gy, 4)

    def partner1(step):
        other = lax.rem(me1 + step, size1)
        return lax.div(other, 4), me2 * 4 + lax.rem(other, 4)

    def partner2(step):
        other = lax.rem(me2 + step, size2)
        return gx, other * 4 + lax.rem(gy, 4)

    barrier = pltpu.get_barrier_semaphore()
    for dx, dy in SIDES:
        pl.semaphore_signal(barrier, inc=1, device_id=device(dx, dy), device_id_type=MESH)

    def greet(step, carry):
        pl.semaphore_signal(barrier, inc=1, device_id=partner1(step), device_id_type=MESH)
        return carry

    def greet2(step, carry):
        pl.semaphore_signal(barrier, inc=1, device_id=partner2(step), device_id_type=MESH)
        return carry

    lax.fori_loop(1, size1, greet, 0)
    lax.fori_loop(1, size2, greet2, 0)

    loads[3].wait()
    own_bc = jnp.concatenate(
        [bc_ref[...].astype(jnp.float32), jnp.zeros((8, 112), jnp.float32)], axis=1
    )
    ba[1] = own_bc
    for slot in range(2):
        for field in range(2):
            for tile in range(2):
                z[slot, field, tile, 0] = zero
                z[slot, field, tile, EX - 1] = zero
    for field in range(2):
        for p in list(range(0, OWN)) + list(range(OWN + CX, EX)):
            rhs[field, p] = zero

    pl.semaphore_wait(barrier, len(SIDES) + size1 - 1 + size2 - 1)
    loads[1].wait()

    first = []

    def push(src, dst, dx, dy):
        n = len(first)
        copy = pltpu.make_async_remote_copy(
            src_ref=src,
            dst_ref=dst,
            send_sem=s1.at[n],
            recv_sem=r1.at[n],
            device_id=device(dx, dy),
            device_id_type=MESH,
        )
        copy.start()
        first.append(copy)

    for dx, dy in SIDES:
        src_x = {0: slice(5, 21), 1: slice(16, 21), -1: slice(5, 10)}[dx]
        dst_x = {0: slice(5, 21), 1: slice(0, 5), -1: slice(21, 26)}[dx]
        y = {0: slice(0, 8), 1: slice(3, 8), -1: slice(0, 5)}[dy]
        half = {0: slice(0, 8), 1: slice(4, 8), -1: slice(0, 4)}[dy]
        place = {0: 1, 1: 0, -1: 2}[dx]
        push(ia.at[src_x, y, :], {0: ia, 1: ip, -1: inn}[dy].at[dst_x, y, :], dx, dy)
        push(ba.at[1, half, :], (bb if dy else ba).at[place, half, :], dx, dy)
    n_ids = len(first)
    loads[0].wait()
    for dx, dy in SIDES:
        src_x = {0: slice(5, 21), 1: slice(17, 21), -1: slice(5, 9)}[dx]
        dst_x = {0: slice(5, 21), 1: slice(1, 5), -1: slice(21, 25)}[dx]
        half = {0: slice(0, 8), 1: slice(4, 8), -1: slice(0, 4)}[dy]
        push(sa.at[:, src_x, half, :], (sb if dy else sa).at[:, dst_x, half, :], dx, dy)

    loads[4].wait()

    def table(row):
        line = jnp.broadcast_to(props_ref[row : row + 1, :], (8, 16))
        return jnp.concatenate([line, jnp.zeros((8, 112), jnp.float32)], axis=1)

    tab_p, tab_t, tab_e = jnp.sqrt(table(0)), jnp.sqrt(table(1)), table(2)

    def look(tab, ids):
        return jnp.take_along_axis(tab, ids, axis=1, mode="promise_in_bounds")

    has_n = (gy < n_gy - 1).astype(jnp.float32)
    has_p = (gy > 0).astype(jnp.float32)

    has_w = (gx > 0).astype(jnp.float32)
    has_e = (gx < n_gx - 1).astype(jnp.float32)
    inside_b = jnp.where(rows < 4, has_n, has_p)

    for copy in first[:n_ids]:
        copy.wait_recv()

    def gather(p):
        inside = ((p >= OWN) | (gx > 0)) & ((p < OWN + CX) | (gx < n_gx - 1))
        inside = inside.astype(jnp.float32)
        id_a, id_n, id_p = ia[p], inn[p], ip[p]
        for f, tab in enumerate((tab_p, tab_t)):
            ga[f, p] = look(tab, id_a) * inside
            n_tile = look(tab, id_n) * (inside * has_n)
            p_tile = look(tab, id_p) * (inside * has_p)
            gn[f, p] = n_tile
            gp[f, p] = p_tile
            gb[f, p] = jnp.where(rows < 4, n_tile, p_tile)
        ea[p] = look(tab_e, id_a)
        eb[p] = jnp.where(rows < 4, look(tab_e, id_n), look(tab_e, id_p))

    def gather_two(p):
        gather(p)
        gather(p + 1)

    planes(0, EX, 2, gather_two)

    loads[2].wait()

    def inverse(g_p, g_t, e, lap_p, lap_t, sto):
        sp, spt, stp, st = sto
        first_ = sp + lap_p
        last = st + lap_t
        cross = stp + e * lap_p
        det = 1.0 / (first_ * last - cross * spt)
        k11 = g_p * (last - e * spt) * det
        k12 = g_p * (e * sp - stp) * det
        k21 = -(g_t * spt) * det
        k22 = g_t * first_ * det
        return k11, k12, k21, k22

    def diagonals(p):
        west = (p < OWN).astype(jnp.int32)
        east = (p >= OWN + CX).astype(jnp.int32)
        place = 1 - west + east
        shift = 127 - (p - OWN + 16 * west - 16 * east)
        top = lanes == 127
        bounds = [jnp.where(top, pltpu.roll(ref[place], shift, 1), 0.0) for ref in (ba, bb)]
        for f in range(2):
            a, b, n_tile, p_tile = ga[f, p], gb[f, p], gn[f, p], gp[f, p]
            a_up, a_down = pltpu.roll(a, 7, 0), pltpu.roll(a, 1, 0)
            b_up, b_down = pltpu.roll(b, 7, 0), pltpu.roll(b, 1, 0)
            y_a = jnp.where(rows == 7, b_up, a_up) + jnp.where(rows == 0, b_down, a_down)
            n_up, n_down = pltpu.roll(n_tile, 7, 0), pltpu.roll(n_tile, 1, 0)
            p_up, p_down = pltpu.roll(p_tile, 7, 0), pltpu.roll(p_tile, 1, 0)
            up = jnp.where(rows < 4, n_up, jnp.where(rows == 7, a_up, p_up))
            down = jnp.where(rows < 4, jnp.where(rows == 0, a_down, n_down), p_down)
            y_b = up + down
            lap_a = a * (ga[f, p - 1] + ga[f, p + 1] + y_a + z_sum(a, lanes))
            lap_b = b * (gb[f, p - 1] + gb[f, p + 1] + y_b + z_sum(b, lanes))
            if f == 0:
                lap_a = lap_a + 2.0 * (a * a) * bounds[0]
                lap_b = lap_b + 2.0 * (b * b) * bounds[1]
            lap[f, 0, p] = lap_a
            lap[f, 1, p] = lap_b

    def invert(p, tile, own):
        g_ref, e_ref, s_ref = ((ga, ea, sa), (gb, eb, sb))[tile]
        g_p, g_t, e = g_ref[0, p], g_ref[1, p], e_ref[p]
        sto = [s_ref[i, p] for i in range(4)]
        k11, k12, k21, k22 = inverse(g_p, g_t, e, lap[0, tile, p], lap[1, tile, p], sto)
        m[0, tile, p] = k11 * g_p
        m[1, tile, p] = k12 * g_t
        m[2, tile, p] = k21 * g_p
        m[3, tile, p] = k22 * g_t
        if own:
            x = p - OWN
            for i, value in enumerate((k11, k12, k21, k22)):
                k_own[i, x] = value
            recip[0, x] = 1.0 / g_p
            recip[1, x] = 1.0 / g_t
            u, t = source[0, x], source[1, x]
            rhs[0, p] = k11 * u + k12 * t
            rhs[1, p] = k21 * u + k22 * t

    planes(1, EX - 1, 2, lambda p: [diagonals(p + i) for i in range(2)])
    planes(OWN, OWN + CX, 4, lambda p: [invert(p + i, 0, True) for i in range(4)])
    for copy in first[n_ids:]:
        copy.wait_recv()
    planes(1, EX - 1, 4, lambda p: [invert(p + i, 1, False) for i in range(4)])
    planes(1, OWN, 4, lambda p: [invert(p + i, 0, False) for i in range(4)])
    planes(OWN + CX, EX - 1, 4, lambda p: [invert(p + i, 0, False) for i in range(4)])

    def solve():
        def start(p):
            for i in range(6):
                for f in range(2):
                    z[0, f, 0, p + i] = rhs[f, p + i]
                    z[0, f, 1, p + i] = zero

        planes(1, EX - 1, 6, start)

        def sweep(index, carry):
            old = lax.rem(index, 2)
            new = 1 - old

            def update(p):
                count = 24
                def load(f, i):
                    return [z[old, f, tile, p + i - 1] for tile in range(2)]

                for i in range(count):
                    sums = []
                    for f in range(2):
                        left, mid, right = load(f, i), load(f, i + 1), load(f, i + 2)
                        sums.append(ring_sum(left, mid[0], mid[1], right, rows, lanes))
                    for tile in range(2):
                        sum_q, sum_t = sums[0][tile], sums[1][tile]
                        for f in range(2):
                            value = (
                                m[2 * f, tile, p + i] * sum_q + m[2 * f + 1, tile, p + i] * sum_t
                            )
                            if tile == 0:
                                value = value + rhs[f, p + i]
                            z[new, f, tile, p + i] = value

            update(1)
            return carry

        lax.fori_loop(0, SWEEPS - 1, sweep, 0)

    last_slot = (SWEEPS - 1) % 2

    def exchange(turn, ssem, rsem):
        copies = []
        for dx, dy in SIDES:
            side = 0 if dx == 1 else 1
            wide = slice(20, 25) if dx == 1 else slice(1, 6)
            narrow = slice(21, 25) if dx == 1 else slice(1, 5)
            narrow_to = slice(1, 5) if dx == 1 else slice(0, 4)
            half = slice(0, 4) if dy == 1 else slice(4, 8)
            line = slice(7, 8) if dy == 1 else slice(0, 1)
            if dy == 0:
                moves = [(z.at[last_slot, :, 0, wide], rx.at[turn, side, :, 0])]
                for edge in (slice(0, 1), slice(7, 8)):
                    moves.append(
                        (
                            z.at[last_slot, :, 1, narrow, edge, :],
                            rx.at[turn, side, :, 1, narrow_to, edge, :],
                        )
                    )
            elif dx == 0:
                moves = [
                    (z.at[last_slot, :, 1, 4:22, half, :], rya.at[turn, :, :, half, :]),
                    (z.at[last_slot, :, 0, 5:21, line, :], ryb.at[turn, :, :, line, :]),
                ]
            else:
                moves = [
                    (z.at[last_slot, :, 1, wide, half, :], rca.at[turn, side, :, :, half, :]),
                    (z.at[last_slot, :, 0, narrow, line, :], rcb.at[turn, side, :, :, line, :]),
                ]
            for src, dst in moves:
                n = len(copies)
                copy = pltpu.make_async_remote_copy(
                    src_ref=src,
                    dst_ref=dst,
                    send_sem=ssem.at[turn, n],
                    recv_sem=rsem.at[turn, n],
                    device_id=device(dx, dy),
                    device_id_type=MESH,
                )
                copy.start()
                copies.append(copy)
        return copies

    def add_up(turn):
        def one(p, west, east):
            for f in range(2):
                a = z[last_slot, f, 0, p] + rya[turn, f, p - 4]
                b = z[last_slot, f, 1, p]
                if west:
                    a = a + (rx[turn, 0, f, 0, p - 4] + rca[turn, 0, f, p - 4])
                if east:
                    a = a + (rx[turn, 1, f, 0, p - 17] + rca[turn, 1, f, p - 17])
                if isinstance(p, int) and p == 4:
                    a = a * has_w
                if isinstance(p, int) and p == 21:
                    a = a * has_e
                fold[f, 0, p - 4] = a
                if not isinstance(p, int) or 5 <= p <= 20:
                    b = b + ryb[turn, f, p - 5]
                    if west:
                        b = b + (rx[turn, 0, f, 1, p - 4] + rcb[turn, 0, f, p - 5])
                    if east:
                        b = b + (rx[turn, 1, f, 1, p - 17] + rcb[turn, 1, f, p - 17])
                    fold[f, 1, p - 4] = b * inside_b

        for p in range(4, 9):
            one(p, True, False)
        planes(9, 17, 4, lambda p: [one(p + i, False, False) for i in range(4)])
        for p in range(17, 22):
            one(p, False, True)

    def apply(turn):
        def one(x, acc):
            i = x + 1
            sums, values = [], []
            for f in range(2):
                a, b = fold[f, 0, i], fold[f, 1, i]
                y_up = jnp.where(rows == 7, pltpu.roll(b, 7, 0), pltpu.roll(a, 7, 0))
                y_down = jnp.where(rows == 0, pltpu.roll(b, 1, 0), pltpu.roll(a, 1, 0))
                near = fold[f, 0, i - 1] + fold[f, 0, i + 1]
                sums.append(near + ((y_up + y_down) + z_sum(a, lanes)))
                values.append(a)
            p = x + OWN
            sp, spt, stp, st = [sa[j, p] for j in range(4)]
            q = values[0] * recip[0, x]
            t = values[1] * recip[1, x]
            u = q - ea[p] * t
            keep_p[turn][0, x] = u
            keep_p[turn][1, x] = t
            w_p = sp * u + lap[0, 0, p] * q + stp * t - ga[0, p] * sums[0]
            w_t = spt * u + (st + lap[1, 0, p]) * t - ga[1, p] * sums[1]
            src_p, src_t = source[0, x], source[1, x]
            if turn == 0:
                d_p, d_t = w_p - src_p, w_t - src_t
                rhs[0, p] = k_own[0, x] * d_p + k_own[1, x] * d_t
                rhs[1, p] = k_own[2, x] * d_p + k_own[3, x] * d_t
                terms = [(src_p, src_t, src_p, src_t), (src_p, src_t, d_p, d_t), (d_p, d_t, d_p, d_t)]
            else:
                o_p, o_t = keep_d[0][0, x], keep_d[0][1, x]
                d_p, d_t = w_p - o_p, w_t - o_t
                terms = [(src_p, src_t, d_p, d_t), (o_p, o_t, d_p, d_t), (d_p, d_t, d_p, d_t)]
            keep_d[turn][0, x] = d_p
            keep_d[turn][1, x] = d_t
            return tuple(
                total + (one_ * two + three * four)
                for total, (one_, three, two, four) in zip(acc, terms)
            )

        def group(index, acc):
            for i in range(4):
                acc = one(index * 4 + i, acc)
            return acc

        return lax.fori_loop(0, CX // 4, group, (zero, zero, zero))

    solve()
    copies = exchange(0, s2, r2)
    for copy in copies:
        copy.wait_recv()
    add_up(0)
    dots_a = apply(0)
    for copy in copies:
        copy.wait_send()
    solve()
    copies = exchange(1, s2, r2)
    for copy in copies:
        copy.wait_recv()
    add_up(1)
    dots_b = apply(1)

    ordered = [dots_a[0], dots_a[1], dots_b[0], dots_a[2], dots_b[1], dots_b[2]]
    tile = zero
    for i, part in enumerate(ordered):
        tile = jnp.where(rows == i, total_rows(part), tile)
    tile = total_rows(jnp.where(rows == lanes, total_lanes(tile), 0.0))[0:1]

    def all_sum(tile, box, me, size, partner, ssem, rsem):
        box[me] = tile

        def copy_of(step):
            return pltpu.make_async_remote_copy(
                src_ref=box.at[me],
                dst_ref=box.at[me],
                send_sem=ssem.at[step],
                recv_sem=rsem.at[step],
                device_id=partner(step),
                device_id_type=MESH,
            )

        def send(step, carry):
            copy_of(step).start()
            return carry

        def receive(step, carry):
            copy_of(step).wait_recv()
            return carry

        lax.fori_loop(1, size, send, 0)
        lax.fori_loop(1, size, receive, 0)
        parts = [box[i] for i in range(size)]
        while len(parts) > 1:
            parts = [parts[i] + parts[i + 1] for i in range(0, len(parts), 2)]
        return parts[0], copy_of

    tile, copy1 = all_sum(tile, g1, me1, size1, partner1, s3, r3)
    tile, copy2 = all_sum(tile, g2, me2, size2, partner2, s4, r4)
    factors = small_problem(total_lanes(jnp.where(rows == lanes, tile, 0.0)), scale)
    table_out = zero
    for i, factor in enumerate(factors):
        table_out = jnp.where(rows == i, factor, table_out)
    factors_ref[...] = table_out

    def drain1(step, carry):
        copy1(step).wait_send()
        return carry

    def drain2(step, carry):
        copy2(step).wait_send()
        return carry

    for copy in first:
        copy.wait_send()
    for copy in copies:
        copy.wait_send()
    lax.fori_loop(1, size1, drain1, 0)
    lax.fori_loop(1, size2, drain2, 0)


def shards(adjoint_source, storage, soil_ids, bc_mask, soil_props):
    f32 = jnp.float32
    cells = 2.0 * 16 * lax.axis_size("gx") * 8 * lax.axis_size("gy") * 128
    out = pltpu.VMEM(adjoint_source.shape, f32)
    any_spec = pl.BlockSpec(memory_space=pltpu.HBM)
    vmem = pl.BlockSpec(memory_space=pltpu.VMEM)

    def buf(*lead, dtype=f32):
        return pltpu.VMEM(tuple(lead) + (8, 128), dtype)

    i32 = jnp.int32
    dma = pltpu.SemaphoreType.DMA
    p1, p2, d1, d2, factors = pl.pallas_call(
        functools.partial(kernel, math.sqrt(cells)),
        out_shape=(out, out, out, out, pltpu.VMEM((8, 128), f32)),
        in_specs=[any_spec] * 5,
        out_specs=(vmem,) * 5,
        scratch_shapes=[
            pltpu.VMEM((8, CX), i32), pltpu.VMEM((3, 16), f32),
            buf(2, CX),
            buf(4, EX), buf(4, EX),
            buf(EX, dtype=i32), buf(EX, dtype=i32), buf(EX, dtype=i32),
            buf(3), buf(3),
            buf(2, EX), buf(2, EX), buf(2, EX), buf(2, EX),
            buf(EX), buf(EX),
            buf(4, 2, EX),
            buf(4, CX), buf(2, 2, EX), buf(2, CX),
            buf(2, EX),
            buf(2, 2, 2, EX),
            buf(2, 2, 18),
            buf(2, 2, 18), buf(2, 2, 16),
            buf(2, 2, 2, 2, 5),
            buf(2, 2, 2, 5), buf(2, 2, 2, 4),
            pltpu.VMEM((32, 1, 128), f32), pltpu.VMEM((8, 1, 128), f32),
            dma((5,)),
            dma((24,)), dma((24,)),
            dma((2, 18)), dma((2, 18)),
            dma((32,)), dma((32,)),
            dma((8,)), dma((8,)),
        ],
        compiler_params=pltpu.CompilerParams(
            collective_id=0, has_side_effects=True, vmem_limit_bytes=60 << 20
        ),
    )(adjoint_source, storage, soil_ids, bc_mask.T, soil_props)
    c = [factors[i] for i in range(8)]
    adjoint = c[0] * p1 + c[1] * p2
    residual = c[2] * adjoint_source + c[3] * d1 + c[4] * d2
    next_basis = c[5] * adjoint_source + c[6] * d1 + c[7] * d2
    return adjoint, residual, next_basis


def solution(mesh):
    in_specs = (
        P(None, "gx", "gy", None),
        P(None, "gx", "gy", None),
        P("gx", "gy", None),
        P("gx", "gy"),
        P(),
    )
    out_specs = (P(None, "gx", "gy", None), P(None, "gx", "gy", None), P(None, "gx", "gy", None))
    return jax.shard_map(shards, mesh=mesh, in_specs=in_specs, out_specs=out_specs, check_vma=False)
```

```python
import functools
import math

import jax
import jax.numpy as jnp
from jax import lax
from jax.experimental import pallas as pl
from jax.experimental.pallas import tpu as pltpu
from jax.sharding import PartitionSpec as P

MESH = pl.DeviceIdType.MESH
CX = 16
EX = 26
OWN = 5
SWEEPS = 6
epsilon = 1e-06


SIDES = [(1, 1), (1, -1), (-1, 1), (-1, -1), (0, 1), (0, -1), (1, 0), (-1, 0)]


def planes(low, high, chunk, body):
    count = (high - low) // chunk

    def group(index, carry):
        body(low + index * chunk)
        return carry

    lax.fori_loop(0, count, group, 0)


def ring_sum(left, a, b, right, rows, lanes):
    a_up, b_up = pltpu.roll(a, 7, 0), pltpu.roll(b, 7, 0)
    a_down, b_down = pltpu.roll(a, 1, 0), pltpu.roll(b, 1, 0)
    y_a = jnp.where(rows == 7, b_up, a_up) + jnp.where(rows == 0, b_down, a_down)
    b_high = jnp.where(rows == 7, a_up, jnp.where(rows == 3, 0.0, b_up))
    b_low = jnp.where(rows == 0, a_down, jnp.where(rows == 4, 0.0, b_down))
    y_b = b_high + b_low
    out_a = (left[0] + right[0]) + (y_a + z_sum(a, lanes))
    out_b = (left[1] + right[1]) + (y_b + z_sum(b, lanes))
    return out_a, out_b


def z_sum(tile, lanes):
    below = jnp.where(lanes == 0, 0.0, pltpu.roll(tile, 1, 1))
    above = jnp.where(lanes == 127, 0.0, pltpu.roll(tile, 127, 1))
    return below + above


def total_rows(tile):
    tile = tile + pltpu.roll(tile, 4, 0)
    tile = tile + pltpu.roll(tile, 2, 0)
    return tile + pltpu.roll(tile, 1, 0)


def total_lanes(tile):
    for shift in (64, 32, 16, 8, 4, 2, 1):
        tile = tile + pltpu.roll(tile, shift, 1)
    return tile


def small_problem(gram, size):
    ss, s1, s2, d11, d12, d22 = [gram[i : i + 1] for i in range(6)]
    square = ss + epsilon
    beta = jnp.sqrt(square)
    g1 = (epsilon - s1) / square
    h11 = 1.0 - g1
    norm1 = (d11 + 2.0 * g1 * s1 + g1 * g1 * ss) / square
    h21 = jnp.sqrt(jnp.maximum(norm1, 0.0) + epsilon)
    al = 1.0 / (beta * h21)
    ga = g1 * al
    h12 = (al * (s1 + s2) + ga * (ss + s1)) / beta
    v22 = al * al * d11 + 2.0 * al * ga * s1 + ga * ga * ss
    e22 = al * (al * d12 + ga * d11) + ga * (al * s2 + ga * s1)
    h22 = v22 + e22
    x3 = al
    x2 = ga + (1.0 - h22) * al
    x1 = (1.0 - h22) * ga - h12 / beta
    norm2 = (
        x3 * x3 * d22
        + x2 * x2 * d11
        + x1 * x1 * ss
        + 2.0 * (x3 * x2 * d12 + x3 * x1 * s2 + x2 * x1 * s1)
    )
    h32 = jnp.sqrt(jnp.maximum(norm2, 0.0) + epsilon)
    r1 = jnp.sqrt(h11 * h11 + h21 * h21)
    c1, n1 = h11 / r1, h21 / r1
    t0, t1 = c1 * beta, -n1 * beta
    u12 = c1 * h12 + n1 * h22
    low = c1 * h22 - n1 * h12
    r2 = jnp.sqrt(low * low + h32 * h32)
    c2 = low / r2
    y2 = c2 * t1 / r2
    y1 = (t0 - u12 * y2) / r1
    f1 = beta - h11 * y1 - h12 * y2
    f2 = -h21 * y1 - h22 * y2
    f3 = -h32 * y2
    a1, a2 = y1 / beta + y2 * ga, y2 * al
    inv = 1.0 / h32
    v31, v32, v33 = x1 * inv, x2 * inv, x3 * inv
    q1 = f1 / beta + f2 * ga + f3 * v31
    q2 = f2 * al + f3 * v32
    q3 = f3 * v33
    return a1, a2, q1, q2, q3, v31 * size, v32 * size, v33 * size


def kernel(
    scale,
    source_hbm, storage_hbm, ids_hbm, bc_hbm, props_hbm,
    p1, p2, d1, d2, factors_ref,
    bc_ref, props_ref, source, sa, sb, ia, inn, ip, ba, bb,
    ga, gb, gn, gp, ea, eb, m, k_own, lap, recip, rhs, z, fold,
    rya, ryb, rx, rca, rcb, g1, g2,
    local_sem, heard, s1, r1, s2, r2, s3, r3, s4, r4,
):
    gx, gy = lax.axis_index("gx"), lax.axis_index("gy")
    n_gx, n_gy = lax.axis_size("gx"), lax.axis_size("gy")
    rows = lax.broadcasted_iota(jnp.int32, (8, 128), 0)
    lanes = lax.broadcasted_iota(jnp.int32, (8, 128), 1)
    zero = jnp.zeros((8, 128), jnp.float32)
    keep_p, keep_d = (p1, p2), (d1, d2)

    def device(dx, dy):
        x = lax.rem(gx + (dx + n_gx), n_gx) if dx else gx
        y = lax.rem(gy + (dy + n_gy), n_gy) if dy else gy
        return x, y

    size1, size2 = n_gx * 4, n_gy // 4
    me1 = gx * 4 + lax.rem(gy, 4)
    me2 = lax.div(gy, 4)

    def partner1(step):
        other = lax.rem(me1 + step, size1)
        return lax.div(other, 4), me2 * 4 + lax.rem(other, 4)

    def partner2(step):
        other = lax.rem(me2 + step, size2)
        return gx, other * 4 + lax.rem(gy, 4)

    barrier = pltpu.get_barrier_semaphore()
    for dx, dy in SIDES:
        pl.semaphore_signal(barrier, inc=1, device_id=device(dx, dy), device_id_type=MESH)

    loads = [
        pltpu.make_async_copy(storage_hbm, sa.at[:, OWN : OWN + CX], local_sem.at[0]),
        pltpu.make_async_copy(ids_hbm, ia.at[OWN : OWN + CX], local_sem.at[1]),
        pltpu.make_async_copy(source_hbm, source, local_sem.at[2]),
        pltpu.make_async_copy(bc_hbm, bc_ref, local_sem.at[3]),
        pltpu.make_async_copy(props_hbm, props_ref, local_sem.at[4]),
    ]
    for copy in loads:
        copy.start()

    loads[3].wait()
    own_bc = jnp.concatenate(
        [bc_ref[...].astype(jnp.float32), jnp.zeros((8, 112), jnp.float32)], axis=1
    )
    ba[1] = own_bc
    for slot in range(2):
        for field in range(2):
            for tile in range(2):
                z[slot, field, tile, 0] = zero
                z[slot, field, tile, EX - 1] = zero
    for field in range(2):
        for p in list(range(0, OWN)) + list(range(OWN + CX, EX)):
            rhs[field, p] = zero

    pl.semaphore_wait(barrier, len(SIDES))
    loads[1].wait()

    first = []

    def push(src, dst, dx, dy):
        n = len(first)
        copy = pltpu.make_async_remote_copy(
            src_ref=src,
            dst_ref=dst,
            send_sem=s1.at[n],
            recv_sem=r1.at[n],
            device_id=device(dx, dy),
            device_id_type=MESH,
        )
        copy.start()
        first.append(copy)

    for dx, dy in SIDES:
        src_x = {0: slice(5, 21), 1: slice(16, 21), -1: slice(5, 10)}[dx]
        dst_x = {0: slice(5, 21), 1: slice(0, 5), -1: slice(21, 26)}[dx]
        y = {0: slice(0, 8), 1: slice(3, 8), -1: slice(0, 5)}[dy]
        half = {0: slice(0, 8), 1: slice(4, 8), -1: slice(0, 4)}[dy]
        place = {0: 1, 1: 0, -1: 2}[dx]
        push(ia.at[src_x, y, :], {0: ia, 1: ip, -1: inn}[dy].at[dst_x, y, :], dx, dy)
        push(ba.at[1, half, :], (bb if dy else ba).at[place, half, :], dx, dy)
    n_ids = len(first)
    loads[0].wait()
    for dx, dy in SIDES[4:6] + SIDES[:4] + SIDES[6:]:
        src_x = {0: slice(5, 21), 1: slice(17, 21), -1: slice(5, 9)}[dx]
        dst_x = {0: slice(5, 21), 1: slice(1, 5), -1: slice(21, 25)}[dx]
        half = {0: slice(0, 8), 1: slice(4, 8), -1: slice(0, 4)}[dy]
        push(sa.at[:, src_x, half, :], (sb if dy else sa).at[:, dst_x, half, :], dx, dy)

    loads[4].wait()

    def table(row):
        line = jnp.broadcast_to(props_ref[row : row + 1, :], (8, 16))
        return jnp.concatenate([line, jnp.zeros((8, 112), jnp.float32)], axis=1)

    tab_p, tab_t, tab_e = jnp.sqrt(table(0)), jnp.sqrt(table(1)), table(2)

    def look(tab, ids):
        return jnp.take_along_axis(tab, ids, axis=1, mode="promise_in_bounds")

    has_n = (gy < n_gy - 1).astype(jnp.float32)
    has_p = (gy > 0).astype(jnp.float32)

    def tell(turn, reach):
        for way in (reach, -reach):
            pl.semaphore_signal(
                heard.at[turn], inc=1, device_id=device(0, way), device_id_type=MESH
            )

    has_w = (gx > 0).astype(jnp.float32)
    has_e = (gx < n_gx - 1).astype(jnp.float32)
    inside_b = jnp.where(rows < 4, has_n, has_p)

    for copy in first[:n_ids]:
        copy.wait_recv()

    def gather(p):
        inside = ((p >= OWN) | (gx > 0)) & ((p < OWN + CX) | (gx < n_gx - 1))
        inside = inside.astype(jnp.float32)
        id_a, id_n, id_p = ia[p], inn[p], ip[p]
        for f, tab in enumerate((tab_p, tab_t)):
            ga[f, p] = look(tab, id_a) * inside
            n_tile = look(tab, id_n) * (inside * has_n)
            p_tile = look(tab, id_p) * (inside * has_p)
            gn[f, p] = n_tile
            gp[f, p] = p_tile
            gb[f, p] = jnp.where(rows < 4, n_tile, p_tile)
        ea[p] = look(tab_e, id_a)
        eb[p] = jnp.where(rows < 4, look(tab_e, id_n), look(tab_e, id_p))

    def gather_two(p):
        gather(p)
        gather(p + 1)

    planes(0, EX, 2, gather_two)

    loads[2].wait()

    def inverse(g_p, g_t, e, lap_p, lap_t, sto):
        sp, spt, stp, st = sto
        first_ = sp + lap_p
        last = st + lap_t
        cross = stp + e * lap_p
        det = 1.0 / (first_ * last - cross * spt)
        k11 = g_p * (last - e * spt) * det
        k12 = g_p * (e * sp - stp) * det
        k21 = -(g_t * spt) * det
        k22 = g_t * first_ * det
        return k11, k12, k21, k22

    def diagonals(p):
        west = (p < OWN).astype(jnp.int32)
        east = (p >= OWN + CX).astype(jnp.int32)
        place = 1 - west + east
        shift = 127 - (p - OWN + 16 * west - 16 * east)
        top = lanes == 127
        bounds = [jnp.where(top, pltpu.roll(ref[place], shift, 1), 0.0) for ref in (ba, bb)]
        for f in range(2):
            a, b, n_tile, p_tile = ga[f, p], gb[f, p], gn[f, p], gp[f, p]
            a_up, a_down = pltpu.roll(a, 7, 0), pltpu.roll(a, 1, 0)
            b_up, b_down = pltpu.roll(b, 7, 0), pltpu.roll(b, 1, 0)
            y_a = jnp.where(rows == 7, b_up, a_up) + jnp.where(rows == 0, b_down, a_down)
            n_up, n_down = pltpu.roll(n_tile, 7, 0), pltpu.roll(n_tile, 1, 0)
            p_up, p_down = pltpu.roll(p_tile, 7, 0), pltpu.roll(p_tile, 1, 0)
            up = jnp.where(rows < 4, n_up, jnp.where(rows == 7, a_up, p_up))
            down = jnp.where(rows < 4, jnp.where(rows == 0, a_down, n_down), p_down)
            y_b = up + down
            lap_a = a * (ga[f, p - 1] + ga[f, p + 1] + y_a + z_sum(a, lanes))
            lap_b = b * (gb[f, p - 1] + gb[f, p + 1] + y_b + z_sum(b, lanes))
            if f == 0:
                lap_a = lap_a + 2.0 * (a * a) * bounds[0]
                lap_b = lap_b + 2.0 * (b * b) * bounds[1]
            lap[f, 0, p] = lap_a
            lap[f, 1, p] = lap_b

    def invert(p, tile, own):
        g_ref, e_ref, s_ref = ((ga, ea, sa), (gb, eb, sb))[tile]
        g_p, g_t, e = g_ref[0, p], g_ref[1, p], e_ref[p]
        sto = [s_ref[i, p] for i in range(4)]
        k11, k12, k21, k22 = inverse(g_p, g_t, e, lap[0, tile, p], lap[1, tile, p], sto)
        m[0, tile, p] = k11 * g_p
        m[1, tile, p] = k12 * g_t
        m[2, tile, p] = k21 * g_p
        m[3, tile, p] = k22 * g_t
        if own:
            x = p - OWN
            for i, value in enumerate((k11, k12, k21, k22)):
                k_own[i, x] = value
            recip[0, x] = 1.0 / g_p
            recip[1, x] = 1.0 / g_t
            u, t = source[0, x], source[1, x]
            rhs[0, p] = k11 * u + k12 * t
            rhs[1, p] = k21 * u + k22 * t

    planes(1, EX - 1, 2, lambda p: [diagonals(p + i) for i in range(2)])
    planes(OWN, OWN + CX, 4, lambda p: [invert(p + i, 0, True) for i in range(4)])
    for copy in first[n_ids:]:
        copy.wait_recv()
    tell(0, 2)
    planes(1, EX - 1, 12, lambda p: [invert(p + i, 1, False) for i in range(12)])
    planes(1, OWN, 4, lambda p: [invert(p + i, 0, False) for i in range(4)])
    planes(OWN + CX, EX - 1, 4, lambda p: [invert(p + i, 0, False) for i in range(4)])

    def solve():
        def start(p):
            for i in range(6):
                for f in range(2):
                    z[0, f, 0, p + i] = rhs[f, p + i]
                    z[0, f, 1, p + i] = zero

        planes(1, EX - 1, 6, start)

        def sweep(index, carry):
            old = lax.rem(index, 2)
            new = 1 - old

            def update(p):
                count = 24
                def load(f, i):
                    return [z[old, f, tile, p + i - 1] for tile in range(2)]

                for i in range(count):
                    sums = []
                    for f in range(2):
                        left, mid, right = load(f, i), load(f, i + 1), load(f, i + 2)
                        sums.append(ring_sum(left, mid[0], mid[1], right, rows, lanes))
                    for tile in range(2):
                        sum_q, sum_t = sums[0][tile], sums[1][tile]
                        for f in range(2):
                            value = (
                                m[2 * f, tile, p + i] * sum_q + m[2 * f + 1, tile, p + i] * sum_t
                            )
                            if tile == 0:
                                value = value + rhs[f, p + i]
                            z[new, f, tile, p + i] = value

            update(1)
            return carry

        lax.fori_loop(0, SWEEPS - 1, sweep, 0)

    last_slot = (SWEEPS - 1) % 2

    def exchange(turn, ssem, rsem):
        copies = []
        for dx, dy in SIDES:
            side = 0 if dx == 1 else 1
            wide = slice(20, 25) if dx == 1 else slice(1, 6)
            narrow = slice(21, 25) if dx == 1 else slice(1, 5)
            narrow_to = slice(1, 5) if dx == 1 else slice(0, 4)
            half = slice(0, 4) if dy == 1 else slice(4, 8)
            line = slice(7, 8) if dy == 1 else slice(0, 1)
            if dy == 0:
                moves = [(z.at[last_slot, :, 0, wide], rx.at[turn, side, :, 0])]
                for edge in (slice(0, 1), slice(7, 8)):
                    moves.append(
                        (
                            z.at[last_slot, :, 1, narrow, edge, :],
                            rx.at[turn, side, :, 1, narrow_to, edge, :],
                        )
                    )
            elif dx == 0:
                moves = [
                    (z.at[last_slot, :, 1, 4:22, half, :], rya.at[turn, :, :, half, :]),
                    (z.at[last_slot, :, 0, 5:21, line, :], ryb.at[turn, :, :, line, :]),
                ]
            else:
                moves = [
                    (z.at[last_slot, :, 1, wide, half, :], rca.at[turn, side, :, :, half, :]),
                    (z.at[last_slot, :, 0, narrow, line, :], rcb.at[turn, side, :, :, line, :]),
                ]
            for src, dst in moves:
                n = len(copies)
                copy = pltpu.make_async_remote_copy(
                    src_ref=src,
                    dst_ref=dst,
                    send_sem=ssem.at[turn, n],
                    recv_sem=rsem.at[turn, n],
                    device_id=device(dx, dy),
                    device_id_type=MESH,
                )
                copy.start()
                copies.append(copy)
        return copies

    def add_up(turn):
        def one(p, west, east):
            for f in range(2):
                a = z[last_slot, f, 0, p] + rya[turn, f, p - 4]
                b = z[last_slot, f, 1, p]
                if west:
                    a = a + (rx[turn, 0, f, 0, p - 4] + rca[turn, 0, f, p - 4])
                if east:
                    a = a + (rx[turn, 1, f, 0, p - 17] + rca[turn, 1, f, p - 17])
                if isinstance(p, int) and p == 4:
                    a = a * has_w
                if isinstance(p, int) and p == 21:
                    a = a * has_e
                fold[f, 0, p - 4] = a
                if not isinstance(p, int) or 5 <= p <= 20:
                    b = b + ryb[turn, f, p - 5]
                    if west:
                        b = b + (rx[turn, 0, f, 1, p - 4] + rcb[turn, 0, f, p - 5])
                    if east:
                        b = b + (rx[turn, 1, f, 1, p - 17] + rcb[turn, 1, f, p - 17])
                    fold[f, 1, p - 4] = b * inside_b

        for p in range(4, 9):
            one(p, True, False)
        planes(9, 17, 8, lambda p: [one(p + i, False, False) for i in range(8)])
        for p in range(17, 22):
            one(p, False, True)

    def apply(turn):
        def one(x, acc):
            i = x + 1
            sums, values = [], []
            for f in range(2):
                a, b = fold[f, 0, i], fold[f, 1, i]
                y_up = jnp.where(rows == 7, pltpu.roll(b, 7, 0), pltpu.roll(a, 7, 0))
                y_down = jnp.where(rows == 0, pltpu.roll(b, 1, 0), pltpu.roll(a, 1, 0))
                near = fold[f, 0, i - 1] + fold[f, 0, i + 1]
                sums.append(near + ((y_up + y_down) + z_sum(a, lanes)))
                values.append(a)
            p = x + OWN
            sp, spt, stp, st = [sa[j, p] for j in range(4)]
            q = values[0] * recip[0, x]
            t = values[1] * recip[1, x]
            u = q - ea[p] * t
            keep_p[turn][0, x] = u
            keep_p[turn][1, x] = t
            w_p = sp * u + lap[0, 0, p] * q + stp * t - ga[0, p] * sums[0]
            w_t = spt * u + (st + lap[1, 0, p]) * t - ga[1, p] * sums[1]
            src_p, src_t = source[0, x], source[1, x]
            if turn == 0:
                d_p, d_t = w_p - src_p, w_t - src_t
                rhs[0, p] = k_own[0, x] * d_p + k_own[1, x] * d_t
                rhs[1, p] = k_own[2, x] * d_p + k_own[3, x] * d_t
                terms = [(src_p, src_t, src_p, src_t), (src_p, src_t, d_p, d_t), (d_p, d_t, d_p, d_t)]
            else:
                o_p, o_t = keep_d[0][0, x], keep_d[0][1, x]
                d_p, d_t = w_p - o_p, w_t - o_t
                terms = [(src_p, src_t, d_p, d_t), (o_p, o_t, d_p, d_t), (d_p, d_t, d_p, d_t)]
            keep_d[turn][0, x] = d_p
            keep_d[turn][1, x] = d_t
            return tuple(
                total + (one_ * two + three * four)
                for total, (one_, three, two, four) in zip(acc, terms)
            )

        def group(index, acc):
            for i in range(8):
                acc = one(index * 8 + i, acc)
            return acc

        return lax.fori_loop(0, CX // 8, group, (zero, zero, zero))

    solve()
    copies = exchange(0, s2, r2)
    for copy in copies:
        copy.wait_recv()
    pl.semaphore_wait(heard.at[0], 2)
    tell(1, 4)
    add_up(0)
    dots_a = apply(0)
    for copy in copies:
        copy.wait_send()
    solve()
    copies = exchange(1, s2, r2)
    for copy in copies:
        copy.wait_recv()
    pl.semaphore_wait(heard.at[1], 2)
    tell(2, 8)
    add_up(1)
    dots_b = apply(1)

    ordered = [dots_a[0], dots_a[1], dots_b[0], dots_a[2], dots_b[1], dots_b[2]]
    tile = zero
    for i, part in enumerate(ordered):
        tile = jnp.where(rows == i, total_rows(part), tile)
    tile = total_rows(jnp.where(rows == lanes, total_lanes(tile), 0.0))[0:1]

    def all_sum(tile, box, me, size, partner, ssem, rsem):
        box[me] = tile

        def copy_of(step):
            return pltpu.make_async_remote_copy(
                src_ref=box.at[me],
                dst_ref=box.at[me],
                send_sem=ssem.at[step],
                recv_sem=rsem.at[step],
                device_id=partner(step),
                device_id_type=MESH,
            )

        def send(step, carry):
            copy_of(step).start()
            return carry

        def receive(step, carry):
            copy_of(step).wait_recv()
            return carry

        lax.fori_loop(1, size, send, 0)
        lax.fori_loop(1, size, receive, 0)
        parts = [box[i] for i in range(size)]
        while len(parts) > 1:
            parts = [parts[i] + parts[i + 1] for i in range(0, len(parts), 2)]
        return parts[0], copy_of

    tile, copy1 = all_sum(tile, g1, me1, size1, partner1, s3, r3)
    pl.semaphore_wait(heard.at[2], 2)
    tile, copy2 = all_sum(tile, g2, me2, size2, partner2, s4, r4)
    factors = small_problem(total_lanes(jnp.where(rows == lanes, tile, 0.0)), scale)
    table_out = zero
    for i, factor in enumerate(factors):
        table_out = jnp.where(rows == i, factor, table_out)
    factors_ref[...] = table_out

    def drain1(step, carry):
        copy1(step).wait_send()
        return carry

    def drain2(step, carry):
        copy2(step).wait_send()
        return carry

    for copy in first:
        copy.wait_send()
    for copy in copies:
        copy.wait_send()
    lax.fori_loop(1, size1, drain1, 0)
    lax.fori_loop(1, size2, drain2, 0)


def shards(adjoint_source, storage, soil_ids, bc_mask, soil_props):
    f32 = jnp.float32
    cells = 2.0 * 16 * lax.axis_size("gx") * 8 * lax.axis_size("gy") * 128
    out = pltpu.VMEM(adjoint_source.shape, f32)
    any_spec = pl.BlockSpec(memory_space=pltpu.HBM)
    vmem = pl.BlockSpec(memory_space=pltpu.VMEM)

    def buf(*lead, dtype=f32):
        return pltpu.VMEM(tuple(lead) + (8, 128), dtype)

    i32 = jnp.int32
    dma = pltpu.SemaphoreType.DMA
    p1, p2, d1, d2, factors = pl.pallas_call(
        functools.partial(kernel, math.sqrt(cells)),
        out_shape=(out, out, out, out, pltpu.VMEM((8, 128), f32)),
        in_specs=[any_spec] * 5,
        out_specs=(vmem,) * 5,
        scratch_shapes=[
            pltpu.VMEM((8, CX), i32), pltpu.VMEM((3, 16), f32),
            buf(2, CX),
            buf(4, EX), buf(4, EX),
            buf(EX, dtype=i32), buf(EX, dtype=i32), buf(EX, dtype=i32),
            buf(3), buf(3),
            buf(2, EX), buf(2, EX), buf(2, EX), buf(2, EX),
            buf(EX), buf(EX),
            buf(4, 2, EX),
            buf(4, CX), buf(2, 2, EX), buf(2, CX),
            buf(2, EX),
            buf(2, 2, 2, EX),
            buf(2, 2, 18),
            buf(2, 2, 18), buf(2, 2, 16),
            buf(2, 2, 2, 2, 5),
            buf(2, 2, 2, 5), buf(2, 2, 2, 4),
            pltpu.VMEM((32, 1, 128), f32), pltpu.VMEM((8, 1, 128), f32),
            dma((5,)), pltpu.SemaphoreType.REGULAR((3,)),
            dma((24,)), dma((24,)),
            dma((2, 18)), dma((2, 18)),
            dma((32,)), dma((32,)),
            dma((8,)), dma((8,)),
        ],
        compiler_params=pltpu.CompilerParams(
            collective_id=0, has_side_effects=True, vmem_limit_bytes=60 << 20
        ),
    )(adjoint_source, storage, soil_ids, bc_mask.T, soil_props)
    c = [factors[i] for i in range(8)]
    adjoint = c[0] * p1 + c[1] * p2
    residual = c[2] * adjoint_source + c[3] * d1 + c[4] * d2
    next_basis = c[5] * adjoint_source + c[6] * d1 + c[7] * d2
    return adjoint, residual, next_basis


def solution(mesh):
    in_specs = (
        P(None, "gx", "gy", None),
        P(None, "gx", "gy", None),
        P("gx", "gy", None),
        P("gx", "gy"),
        P(),
    )
    out_specs = (P(None, "gx", "gy", None), P(None, "gx", "gy", None), P(None, "gx", "gy", None))
    return jax.shard_map(shards, mesh=mesh, in_specs=in_specs, out_specs=out_specs, check_vma=False)
```

```python
import functools
import math

import jax
import jax.numpy as jnp
from jax import lax
from jax.experimental import pallas as pl
from jax.experimental.pallas import tpu as pltpu
from jax.sharding import PartitionSpec as P

MESH = pl.DeviceIdType.MESH
CX = 16
EX = 26
OWN = 5
SWEEPS = 6
epsilon = 1e-06


SIDES = [(1, 1), (1, -1), (-1, 1), (-1, -1), (0, 1), (0, -1), (1, 0), (-1, 0)]


def planes(low, high, chunk, body):
    count = (high - low) // chunk

    def group(index, carry):
        body(low + index * chunk)
        return carry

    lax.fori_loop(0, count, group, 0)


def ring_sum(left, a, b, right, rows, lanes):
    a_up, b_up = pltpu.roll(a, 7, 0), pltpu.roll(b, 7, 0)
    a_down, b_down = pltpu.roll(a, 1, 0), pltpu.roll(b, 1, 0)
    y_a = jnp.where(rows == 7, b_up, a_up) + jnp.where(rows == 0, b_down, a_down)
    b_high = jnp.where(rows == 7, a_up, jnp.where(rows == 3, 0.0, b_up))
    b_low = jnp.where(rows == 0, a_down, jnp.where(rows == 4, 0.0, b_down))
    y_b = b_high + b_low
    out_a = (left[0] + right[0]) + (y_a + z_sum(a, lanes))
    out_b = (left[1] + right[1]) + (y_b + z_sum(b, lanes))
    return out_a, out_b


def z_sum(tile, lanes):
    below = jnp.where(lanes == 0, 0.0, pltpu.roll(tile, 1, 1))
    above = jnp.where(lanes == 127, 0.0, pltpu.roll(tile, 127, 1))
    return below + above


def total_rows(tile):
    tile = tile + pltpu.roll(tile, 4, 0)
    tile = tile + pltpu.roll(tile, 2, 0)
    return tile + pltpu.roll(tile, 1, 0)


def total_lanes(tile):
    for shift in (64, 32, 16, 8, 4, 2, 1):
        tile = tile + pltpu.roll(tile, shift, 1)
    return tile


def small_problem(gram, size):
    ss, s1, s2, d11, d12, d22 = [gram[i : i + 1] for i in range(6)]
    square = ss + epsilon
    beta = jnp.sqrt(square)
    g1 = (epsilon - s1) / square
    h11 = 1.0 - g1
    norm1 = (d11 + 2.0 * g1 * s1 + g1 * g1 * ss) / square
    h21 = jnp.sqrt(jnp.maximum(norm1, 0.0) + epsilon)
    al = 1.0 / (beta * h21)
    ga = g1 * al
    h12 = (al * (s1 + s2) + ga * (ss + s1)) / beta
    v22 = al * al * d11 + 2.0 * al * ga * s1 + ga * ga * ss
    e22 = al * (al * d12 + ga * d11) + ga * (al * s2 + ga * s1)
    h22 = v22 + e22
    x3 = al
    x2 = ga + (1.0 - h22) * al
    x1 = (1.0 - h22) * ga - h12 / beta
    norm2 = (
        x3 * x3 * d22
        + x2 * x2 * d11
        + x1 * x1 * ss
        + 2.0 * (x3 * x2 * d12 + x3 * x1 * s2 + x2 * x1 * s1)
    )
    h32 = jnp.sqrt(jnp.maximum(norm2, 0.0) + epsilon)
    r1 = jnp.sqrt(h11 * h11 + h21 * h21)
    c1, n1 = h11 / r1, h21 / r1
    t0, t1 = c1 * beta, -n1 * beta
    u12 = c1 * h12 + n1 * h22
    low = c1 * h22 - n1 * h12
    r2 = jnp.sqrt(low * low + h32 * h32)
    c2 = low / r2
    y2 = c2 * t1 / r2
    y1 = (t0 - u12 * y2) / r1
    f1 = beta - h11 * y1 - h12 * y2
    f2 = -h21 * y1 - h22 * y2
    f3 = -h32 * y2
    a1, a2 = y1 / beta + y2 * ga, y2 * al
    inv = 1.0 / h32
    v31, v32, v33 = x1 * inv, x2 * inv, x3 * inv
    q1 = f1 / beta + f2 * ga + f3 * v31
    q2 = f2 * al + f3 * v32
    q3 = f3 * v33
    return a1, a2, q1, q2, q3, v31 * size, v32 * size, v33 * size


def kernel(
    scale,
    source_hbm, storage_hbm, ids_hbm, bc_hbm, props_hbm,
    p1, p2, d1, d2, factors_ref,
    bc_ref, props_ref, source, sa, sb, ia, inn, ip, ba, bb,
    ga, gb, gn, gp, ea, eb, m, k_own, lap, recip, rhs, z, fold,
    rya, ryb, rx, rca, rcb, g1, g2,
    local_sem, heard, s1, r1, s2, r2, s3, r3, s4, r4,
):
    gx, gy = lax.axis_index("gx"), lax.axis_index("gy")
    n_gx, n_gy = lax.axis_size("gx"), lax.axis_size("gy")
    rows = lax.broadcasted_iota(jnp.int32, (8, 128), 0)
    lanes = lax.broadcasted_iota(jnp.int32, (8, 128), 1)
    zero = jnp.zeros((8, 128), jnp.float32)
    keep_p, keep_d = (p1, p2), (d1, d2)

    def device(dx, dy):
        x = lax.rem(gx + (dx + n_gx), n_gx) if dx else gx
        y = lax.rem(gy + (dy + n_gy), n_gy) if dy else gy
        return x, y

    size1, size2 = n_gx * 4, n_gy // 4
    me1 = gx * 4 + lax.rem(gy, 4)
    me2 = lax.div(gy, 4)

    def partner1(step):
        other = lax.rem(me1 + step, size1)
        return lax.div(other, 4), me2 * 4 + lax.rem(other, 4)

    def partner2(step):
        other = lax.rem(me2 + step, size2)
        return gx, other * 4 + lax.rem(gy, 4)

    barrier = pltpu.get_barrier_semaphore()
    for dx, dy in SIDES:
        pl.semaphore_signal(barrier, inc=1, device_id=device(dx, dy), device_id_type=MESH)

    loads = [
        pltpu.make_async_copy(storage_hbm, sa.at[:, OWN : OWN + CX], local_sem.at[0]),
        pltpu.make_async_copy(ids_hbm, ia.at[OWN : OWN + CX], local_sem.at[1]),
        pltpu.make_async_copy(source_hbm, source, local_sem.at[2]),
        pltpu.make_async_copy(bc_hbm, bc_ref, local_sem.at[3]),
        pltpu.make_async_copy(props_hbm, props_ref, local_sem.at[4]),
    ]
    for copy in loads:
        copy.start()

    loads[3].wait()
    own_bc = jnp.concatenate(
        [bc_ref[...].astype(jnp.float32), jnp.zeros((8, 112), jnp.float32)], axis=1
    )
    ba[1] = own_bc
    for slot in range(2):
        for field in range(2):
            for tile in range(2):
                z[slot, field, tile, 0] = zero
                z[slot, field, tile, EX - 1] = zero
    for field in range(2):
        for p in list(range(0, OWN)) + list(range(OWN + CX, EX)):
            rhs[field, p] = zero

    pl.semaphore_wait(barrier, len(SIDES))
    loads[1].wait()

    first = []

    def push(src, dst, dx, dy):
        n = len(first)
        copy = pltpu.make_async_remote_copy(
            src_ref=src,
            dst_ref=dst,
            send_sem=s1.at[n],
            recv_sem=r1.at[n],
            device_id=device(dx, dy),
            device_id_type=MESH,
        )
        copy.start()
        first.append(copy)

    for dx, dy in SIDES:
        src_x = {0: slice(5, 21), 1: slice(16, 21), -1: slice(5, 10)}[dx]
        dst_x = {0: slice(5, 21), 1: slice(0, 5), -1: slice(21, 26)}[dx]
        y = {0: slice(0, 8), 1: slice(3, 8), -1: slice(0, 5)}[dy]
        half = {0: slice(0, 8), 1: slice(4, 8), -1: slice(0, 4)}[dy]
        place = {0: 1, 1: 0, -1: 2}[dx]
        push(ia.at[src_x, y, :], {0: ia, 1: ip, -1: inn}[dy].at[dst_x, y, :], dx, dy)
        push(ba.at[1, half, :], (bb if dy else ba).at[place, half, :], dx, dy)
    n_ids = len(first)
    loads[0].wait()
    for dx, dy in SIDES[4:6] + SIDES[:4] + SIDES[6:]:
        src_x = {0: slice(5, 21), 1: slice(17, 21), -1: slice(5, 9)}[dx]
        dst_x = {0: slice(5, 21), 1: slice(1, 5), -1: slice(21, 25)}[dx]
        half = {0: slice(0, 8), 1: slice(4, 8), -1: slice(0, 4)}[dy]
        push(sa.at[:, src_x, half, :], (sb if dy else sa).at[:, dst_x, half, :], dx, dy)

    loads[4].wait()

    def table(row):
        line = jnp.broadcast_to(props_ref[row : row + 1, :], (8, 16))
        return jnp.concatenate([line, jnp.zeros((8, 112), jnp.float32)], axis=1)

    tab_p, tab_t, tab_e = jnp.sqrt(table(0)), jnp.sqrt(table(1)), table(2)

    def look(tab, ids):
        return jnp.take_along_axis(tab, ids, axis=1, mode="promise_in_bounds")

    has_n = (gy < n_gy - 1).astype(jnp.float32)
    has_p = (gy > 0).astype(jnp.float32)

    def tell(turn, reach):
        for way in (reach, -reach):
            pl.semaphore_signal(
                heard.at[turn], inc=1, device_id=device(0, way), device_id_type=MESH
            )

    has_w = (gx > 0).astype(jnp.float32)
    has_e = (gx < n_gx - 1).astype(jnp.float32)
    inside_b = jnp.where(rows < 4, has_n, has_p)

    for copy in first[:n_ids]:
        copy.wait_recv()

    def gather(p):
        inside = ((p >= OWN) | (gx > 0)) & ((p < OWN + CX) | (gx < n_gx - 1))
        inside = inside.astype(jnp.float32)
        id_a, id_n, id_p = ia[p], inn[p], ip[p]
        for f, tab in enumerate((tab_p, tab_t)):
            ga[f, p] = look(tab, id_a) * inside
            n_tile = look(tab, id_n) * (inside * has_n)
            p_tile = look(tab, id_p) * (inside * has_p)
            gn[f, p] = n_tile
            gp[f, p] = p_tile
            gb[f, p] = jnp.where(rows < 4, n_tile, p_tile)
        ea[p] = look(tab_e, id_a)
        eb[p] = jnp.where(rows < 4, look(tab_e, id_n), look(tab_e, id_p))

    planes(0, EX, 13, lambda p: [gather(p + i) for i in range(13)])

    loads[2].wait()

    def inverse(g_p, g_t, e, lap_p, lap_t, sto):
        sp, spt, stp, st = sto
        first_ = sp + lap_p
        last = st + lap_t
        cross = stp + e * lap_p
        det = 1.0 / (first_ * last - cross * spt)
        k11 = g_p * (last - e * spt) * det
        k12 = g_p * (e * sp - stp) * det
        k21 = -(g_t * spt) * det
        k22 = g_t * first_ * det
        return k11, k12, k21, k22

    def diagonals(p):
        west = (p < OWN).astype(jnp.int32)
        east = (p >= OWN + CX).astype(jnp.int32)
        place = 1 - west + east
        shift = 127 - (p - OWN + 16 * west - 16 * east)
        top = lanes == 127
        bounds = [jnp.where(top, pltpu.roll(ref[place], shift, 1), 0.0) for ref in (ba, bb)]
        for f in range(2):
            a, b, n_tile, p_tile = ga[f, p], gb[f, p], gn[f, p], gp[f, p]
            a_up, a_down = pltpu.roll(a, 7, 0), pltpu.roll(a, 1, 0)
            b_up, b_down = pltpu.roll(b, 7, 0), pltpu.roll(b, 1, 0)
            y_a = jnp.where(rows == 7, b_up, a_up) + jnp.where(rows == 0, b_down, a_down)
            n_up, n_down = pltpu.roll(n_tile, 7, 0), pltpu.roll(n_tile, 1, 0)
            p_up, p_down = pltpu.roll(p_tile, 7, 0), pltpu.roll(p_tile, 1, 0)
            up = jnp.where(rows < 4, n_up, jnp.where(rows == 7, a_up, p_up))
            down = jnp.where(rows < 4, jnp.where(rows == 0, a_down, n_down), p_down)
            y_b = up + down
            lap_a = a * (ga[f, p - 1] + ga[f, p + 1] + y_a + z_sum(a, lanes))
            lap_b = b * (gb[f, p - 1] + gb[f, p + 1] + y_b + z_sum(b, lanes))
            if f == 0:
                lap_a = lap_a + 2.0 * (a * a) * bounds[0]
                lap_b = lap_b + 2.0 * (b * b) * bounds[1]
            lap[f, 0, p] = lap_a
            lap[f, 1, p] = lap_b

    def invert(p, tile, own):
        g_ref, e_ref, s_ref = ((ga, ea, sa), (gb, eb, sb))[tile]
        g_p, g_t, e = g_ref[0, p], g_ref[1, p], e_ref[p]
        sto = [s_ref[i, p] for i in range(4)]
        k11, k12, k21, k22 = inverse(g_p, g_t, e, lap[0, tile, p], lap[1, tile, p], sto)
        m[0, tile, p] = k11 * g_p
        m[1, tile, p] = k12 * g_t
        m[2, tile, p] = k21 * g_p
        m[3, tile, p] = k22 * g_t
        if own:
            x = p - OWN
            for i, value in enumerate((k11, k12, k21, k22)):
                k_own[i, x] = value
            recip[0, x] = 1.0 / g_p
            recip[1, x] = 1.0 / g_t
            u, t = source[0, x], source[1, x]
            rhs[0, p] = k11 * u + k12 * t
            rhs[1, p] = k21 * u + k22 * t

    planes(1, EX - 1, 24, lambda p: [diagonals(p + i) for i in range(24)])
    planes(OWN, OWN + CX, 8, lambda p: [invert(p + i, 0, True) for i in range(8)])
    for copy in first[n_ids:]:
        copy.wait_recv()
    tell(0, 2)
    planes(1, EX - 1, 24, lambda p: [invert(p + i, 1, False) for i in range(24)])
    planes(1, OWN, 4, lambda p: [invert(p + i, 0, False) for i in range(4)])
    planes(OWN + CX, EX - 1, 4, lambda p: [invert(p + i, 0, False) for i in range(4)])

    def solve():
        def start(p):
            for i in range(6):
                for f in range(2):
                    z[0, f, 0, p + i] = rhs[f, p + i]
                    z[0, f, 1, p + i] = zero

        planes(1, EX - 1, 6, start)

        def sweep(index, carry):
            old = lax.rem(index, 2)
            new = 1 - old

            def update(p):
                count = 24
                def load(f, i):
                    return [z[old, f, tile, p + i - 1] for tile in range(2)]

                for i in range(count):
                    sums = []
                    for f in range(2):
                        left, mid, right = load(f, i), load(f, i + 1), load(f, i + 2)
                        sums.append(ring_sum(left, mid[0], mid[1], right, rows, lanes))
                    for tile in range(2):
                        sum_q, sum_t = sums[0][tile], sums[1][tile]
                        for f in range(2):
                            value = (
                                m[2 * f, tile, p + i] * sum_q + m[2 * f + 1, tile, p + i] * sum_t
                            )
                            if tile == 0:
                                value = value + rhs[f, p + i]
                            z[new, f, tile, p + i] = value

            update(1)
            return carry

        lax.fori_loop(0, SWEEPS - 1, sweep, 0)

    last_slot = (SWEEPS - 1) % 2

    def exchange(turn, ssem, rsem):
        copies = []
        for dx, dy in SIDES:
            side = 0 if dx == 1 else 1
            wide = slice(20, 25) if dx == 1 else slice(1, 6)
            narrow = slice(21, 25) if dx == 1 else slice(1, 5)
            narrow_to = slice(1, 5) if dx == 1 else slice(0, 4)
            half = slice(0, 4) if dy == 1 else slice(4, 8)
            line = slice(7, 8) if dy == 1 else slice(0, 1)
            if dy == 0:
                moves = [(z.at[last_slot, :, 0, wide], rx.at[turn, side, :, 0])]
                for edge in (slice(0, 1), slice(7, 8)):
                    moves.append(
                        (
                            z.at[last_slot, :, 1, narrow, edge, :],
                            rx.at[turn, side, :, 1, narrow_to, edge, :],
                        )
                    )
            elif dx == 0:
                moves = [
                    (z.at[last_slot, :, 1, 4:22, half, :], rya.at[turn, :, :, half, :]),
                    (z.at[last_slot, :, 0, 5:21, line, :], ryb.at[turn, :, :, line, :]),
                ]
            else:
                moves = [
                    (z.at[last_slot, :, 1, wide, half, :], rca.at[turn, side, :, :, half, :]),
                    (z.at[last_slot, :, 0, narrow, line, :], rcb.at[turn, side, :, :, line, :]),
                ]
            for src, dst in moves:
                n = len(copies)
                copy = pltpu.make_async_remote_copy(
                    src_ref=src,
                    dst_ref=dst,
                    send_sem=ssem.at[turn, n],
                    recv_sem=rsem.at[turn, n],
                    device_id=device(dx, dy),
                    device_id_type=MESH,
                )
                copy.start()
                copies.append(copy)
        return copies

    def add_up(turn):
        def one(p, west, east):
            for f in range(2):
                a = z[last_slot, f, 0, p] + rya[turn, f, p - 4]
                b = z[last_slot, f, 1, p]
                if west:
                    a = a + (rx[turn, 0, f, 0, p - 4] + rca[turn, 0, f, p - 4])
                if east:
                    a = a + (rx[turn, 1, f, 0, p - 17] + rca[turn, 1, f, p - 17])
                if isinstance(p, int) and p == 4:
                    a = a * has_w
                if isinstance(p, int) and p == 21:
                    a = a * has_e
                fold[f, 0, p - 4] = a
                if not isinstance(p, int) or 5 <= p <= 20:
                    b = b + ryb[turn, f, p - 5]
                    if west:
                        b = b + (rx[turn, 0, f, 1, p - 4] + rcb[turn, 0, f, p - 5])
                    if east:
                        b = b + (rx[turn, 1, f, 1, p - 17] + rcb[turn, 1, f, p - 17])
                    fold[f, 1, p - 4] = b * inside_b

        for p in range(4, 9):
            one(p, True, False)
        planes(9, 17, 8, lambda p: [one(p + i, False, False) for i in range(8)])
        for p in range(17, 22):
            one(p, False, True)

    def apply(turn):
        def one(x, acc):
            i = x + 1
            sums, values = [], []
            for f in range(2):
                a, b = fold[f, 0, i], fold[f, 1, i]
                y_up = jnp.where(rows == 7, pltpu.roll(b, 7, 0), pltpu.roll(a, 7, 0))
                y_down = jnp.where(rows == 0, pltpu.roll(b, 1, 0), pltpu.roll(a, 1, 0))
                near = fold[f, 0, i - 1] + fold[f, 0, i + 1]
                sums.append(near + ((y_up + y_down) + z_sum(a, lanes)))
                values.append(a)
            p = x + OWN
            sp, spt, stp, st = [sa[j, p] for j in range(4)]
            q = values[0] * recip[0, x]
            t = values[1] * recip[1, x]
            u = q - ea[p] * t
            keep_p[turn][0, x] = u
            keep_p[turn][1, x] = t
            w_p = sp * u + lap[0, 0, p] * q + stp * t - ga[0, p] * sums[0]
            w_t = spt * u + (st + lap[1, 0, p]) * t - ga[1, p] * sums[1]
            src_p, src_t = source[0, x], source[1, x]
            if turn == 0:
                d_p, d_t = w_p - src_p, w_t - src_t
                rhs[0, p] = k_own[0, x] * d_p + k_own[1, x] * d_t
                rhs[1, p] = k_own[2, x] * d_p + k_own[3, x] * d_t
                terms = [(src_p, src_t, src_p, src_t), (src_p, src_t, d_p, d_t), (d_p, d_t, d_p, d_t)]
            else:
                o_p, o_t = keep_d[0][0, x], keep_d[0][1, x]
                d_p, d_t = w_p - o_p, w_t - o_t
                terms = [(src_p, src_t, d_p, d_t), (o_p, o_t, d_p, d_t), (d_p, d_t, d_p, d_t)]
            keep_d[turn][0, x] = d_p
            keep_d[turn][1, x] = d_t
            return tuple(
                total + (one_ * two + three * four)
                for total, (one_, three, two, four) in zip(acc, terms)
            )

        def group(index, acc):
            for i in range(16):
                acc = one(index * 16 + i, acc)
            return acc

        return lax.fori_loop(0, CX // 16, group, (zero, zero, zero))

    solve()
    copies = exchange(0, s2, r2)
    for copy in copies:
        copy.wait_recv()
    pl.semaphore_wait(heard.at[0], 2)
    tell(1, 4)
    add_up(0)
    dots_a = apply(0)
    for copy in copies:
        copy.wait_send()
    solve()
    copies = exchange(1, s2, r2)
    for copy in copies:
        copy.wait_recv()
    pl.semaphore_wait(heard.at[1], 2)
    tell(2, 8)
    add_up(1)
    dots_b = apply(1)

    ordered = [dots_a[0], dots_a[1], dots_b[0], dots_a[2], dots_b[1], dots_b[2]]
    tile = zero
    for i, part in enumerate(ordered):
        tile = jnp.where(rows == i, total_rows(part), tile)
    tile = total_rows(jnp.where(rows == lanes, total_lanes(tile), 0.0))[0:1]

    def all_sum(tile, box, me, size, partner, ssem, rsem):
        box[me] = tile

        def copy_of(step):
            return pltpu.make_async_remote_copy(
                src_ref=box.at[me],
                dst_ref=box.at[me],
                send_sem=ssem.at[step],
                recv_sem=rsem.at[step],
                device_id=partner(step),
                device_id_type=MESH,
            )

        def send(step, carry):
            copy_of(step).start()
            return carry

        def receive(step, carry):
            copy_of(step).wait_recv()
            return carry

        for step in range(1, size):
            send(step, 0)
        lax.fori_loop(1, size, receive, 0)
        parts = [box[i] for i in range(size)]
        while len(parts) > 1:
            parts = [parts[i] + parts[i + 1] for i in range(0, len(parts), 2)]
        return parts[0], copy_of

    tile, copy1 = all_sum(tile, g1, me1, size1, partner1, s3, r3)
    pl.semaphore_wait(heard.at[2], 2)
    tile, copy2 = all_sum(tile, g2, me2, size2, partner2, s4, r4)
    factors = small_problem(total_lanes(jnp.where(rows == lanes, tile, 0.0)), scale)
    table_out = zero
    for i, factor in enumerate(factors):
        table_out = jnp.where(rows == i, factor, table_out)
    factors_ref[...] = table_out

    def drain1(step, carry):
        copy1(step).wait_send()
        return carry

    def drain2(step, carry):
        copy2(step).wait_send()
        return carry

    for copy in first:
        copy.wait_send()
    for copy in copies:
        copy.wait_send()
    lax.fori_loop(1, size1, drain1, 0)
    lax.fori_loop(1, size2, drain2, 0)


def shards(adjoint_source, storage, soil_ids, bc_mask, soil_props):
    f32 = jnp.float32
    cells = 2.0 * 16 * lax.axis_size("gx") * 8 * lax.axis_size("gy") * 128
    out = pltpu.VMEM(adjoint_source.shape, f32)
    any_spec = pl.BlockSpec(memory_space=pltpu.HBM)
    vmem = pl.BlockSpec(memory_space=pltpu.VMEM)

    def buf(*lead, dtype=f32):
        return pltpu.VMEM(tuple(lead) + (8, 128), dtype)

    i32 = jnp.int32
    dma = pltpu.SemaphoreType.DMA
    p1, p2, d1, d2, factors = pl.pallas_call(
        functools.partial(kernel, math.sqrt(cells)),
        out_shape=(out, out, out, out, pltpu.VMEM((8, 128), f32)),
        in_specs=[any_spec] * 5,
        out_specs=(vmem,) * 5,
        scratch_shapes=[
            pltpu.VMEM((8, CX), i32), pltpu.VMEM((3, 16), f32),
            buf(2, CX),
            buf(4, EX), buf(4, EX),
            buf(EX, dtype=i32), buf(EX, dtype=i32), buf(EX, dtype=i32),
            buf(3), buf(3),
            buf(2, EX), buf(2, EX), buf(2, EX), buf(2, EX),
            buf(EX), buf(EX),
            buf(4, 2, EX),
            buf(4, CX), buf(2, 2, EX), buf(2, CX),
            buf(2, EX),
            buf(2, 2, 2, EX),
            buf(2, 2, 18),
            buf(2, 2, 18), buf(2, 2, 16),
            buf(2, 2, 2, 2, 5),
            buf(2, 2, 2, 5), buf(2, 2, 2, 4),
            pltpu.VMEM((32, 1, 128), f32), pltpu.VMEM((8, 1, 128), f32),
            dma((5,)), pltpu.SemaphoreType.REGULAR((3,)),
            dma((24,)), dma((24,)),
            dma((2, 18)), dma((2, 18)),
            dma((32,)), dma((32,)),
            dma((8,)), dma((8,)),
        ],
        compiler_params=pltpu.CompilerParams(
            collective_id=0, has_side_effects=True, vmem_limit_bytes=60 << 20
        ),
    )(adjoint_source, storage, soil_ids, bc_mask.T, soil_props)
    c = [factors[i] for i in range(8)]
    adjoint = c[0] * p1 + c[1] * p2
    residual = c[2] * adjoint_source + c[3] * d1 + c[4] * d2
    next_basis = c[5] * adjoint_source + c[6] * d1 + c[7] * d2
    return adjoint, residual, next_basis


def solution(mesh):
    in_specs = (
        P(None, "gx", "gy", None),
        P(None, "gx", "gy", None),
        P("gx", "gy", None),
        P("gx", "gy"),
        P(),
    )
    out_specs = (P(None, "gx", "gy", None), P(None, "gx", "gy", None), P(None, "gx", "gy", None))
    return jax.shard_map(shards, mesh=mesh, in_specs=in_specs, out_specs=out_specs, check_vma=False)
```

```python
import functools
import math

import jax
import jax.numpy as jnp
from jax import lax
from jax.experimental import pallas as pl
from jax.experimental.pallas import tpu as pltpu
from jax.sharding import PartitionSpec as P

MESH = pl.DeviceIdType.MESH
CX = 16
EX = 26
OWN = 5
SWEEPS = 6
epsilon = 1e-06


SIDES = [(1, 1), (1, -1), (-1, 1), (-1, -1), (0, 1), (0, -1), (1, 0), (-1, 0)]


def planes(low, high, chunk, body):
    count = (high - low) // chunk

    def group(index, carry):
        body(low + index * chunk)
        return carry

    lax.fori_loop(0, count, group, 0)


def ring_sum(left, a, b, right, rows, lanes):
    a_up, b_up = pltpu.roll(a, 7, 0), pltpu.roll(b, 7, 0)
    a_down, b_down = pltpu.roll(a, 1, 0), pltpu.roll(b, 1, 0)
    y_a = jnp.where(rows == 7, b_up, a_up) + jnp.where(rows == 0, b_down, a_down)
    b_high = jnp.where(rows == 7, a_up, jnp.where(rows == 3, 0.0, b_up))
    b_low = jnp.where(rows == 0, a_down, jnp.where(rows == 4, 0.0, b_down))
    y_b = b_high + b_low
    out_a = (left[0] + right[0]) + (y_a + z_sum(a, lanes))
    out_b = (left[1] + right[1]) + (y_b + z_sum(b, lanes))
    return out_a, out_b


def z_sum(tile, lanes):
    below = jnp.where(lanes == 0, 0.0, pltpu.roll(tile, 1, 1))
    above = jnp.where(lanes == 127, 0.0, pltpu.roll(tile, 127, 1))
    return below + above


def total_rows(tile):
    tile = tile + pltpu.roll(tile, 4, 0)
    tile = tile + pltpu.roll(tile, 2, 0)
    return tile + pltpu.roll(tile, 1, 0)


def total_lanes(tile):
    for shift in (64, 32, 16, 8, 4, 2, 1):
        tile = tile + pltpu.roll(tile, shift, 1)
    return tile


def small_problem(gram, size):
    ss, s1, s2, d11, d12, d22 = [gram[i : i + 1] for i in range(6)]
    square = ss + epsilon
    beta = jnp.sqrt(square)
    g1 = (epsilon - s1) / square
    h11 = 1.0 - g1
    norm1 = (d11 + 2.0 * g1 * s1 + g1 * g1 * ss) / square
    h21 = jnp.sqrt(jnp.maximum(norm1, 0.0) + epsilon)
    al = 1.0 / (beta * h21)
    ga = g1 * al
    h12 = (al * (s1 + s2) + ga * (ss + s1)) / beta
    v22 = al * al * d11 + 2.0 * al * ga * s1 + ga * ga * ss
    e22 = al * (al * d12 + ga * d11) + ga * (al * s2 + ga * s1)
    h22 = v22 + e22
    x3 = al
    x2 = ga + (1.0 - h22) * al
    x1 = (1.0 - h22) * ga - h12 / beta
    norm2 = (
        x3 * x3 * d22
        + x2 * x2 * d11
        + x1 * x1 * ss
        + 2.0 * (x3 * x2 * d12 + x3 * x1 * s2 + x2 * x1 * s1)
    )
    h32 = jnp.sqrt(jnp.maximum(norm2, 0.0) + epsilon)
    r1 = jnp.sqrt(h11 * h11 + h21 * h21)
    c1, n1 = h11 / r1, h21 / r1
    t0, t1 = c1 * beta, -n1 * beta
    u12 = c1 * h12 + n1 * h22
    low = c1 * h22 - n1 * h12
    r2 = jnp.sqrt(low * low + h32 * h32)
    c2 = low / r2
    y2 = c2 * t1 / r2
    y1 = (t0 - u12 * y2) / r1
    f1 = beta - h11 * y1 - h12 * y2
    f2 = -h21 * y1 - h22 * y2
    f3 = -h32 * y2
    a1, a2 = y1 / beta + y2 * ga, y2 * al
    inv = 1.0 / h32
    v31, v32, v33 = x1 * inv, x2 * inv, x3 * inv
    q1 = f1 / beta + f2 * ga + f3 * v31
    q2 = f2 * al + f3 * v32
    q3 = f3 * v33
    return a1, a2, q1, q2, q3, v31 * size, v32 * size, v33 * size


def kernel(
    scale,
    source_hbm, storage_hbm, ids_hbm, bc_hbm, props_hbm,
    p1, p2, d1, d2, factors_ref,
    bc_ref, props_ref, source, sa, sb, ia, inn, ip, ba, bb,
    ga, gb, gn, gp, ea, eb, m, k_own, lap, recip, rhs, z, fold,
    rya, ryb, rx, rca, rcb, g1, g2,
    local_sem, heard, s1, r1, s2, r2, s3, r3, s4, r4,
):
    gx, gy = lax.axis_index("gx"), lax.axis_index("gy")
    n_gx, n_gy = lax.axis_size("gx"), lax.axis_size("gy")
    rows = lax.broadcasted_iota(jnp.int32, (8, 128), 0)
    lanes = lax.broadcasted_iota(jnp.int32, (8, 128), 1)
    zero = jnp.zeros((8, 128), jnp.float32)
    keep_p, keep_d = (p1, p2), (d1, d2)

    def device(dx, dy):
        x = lax.rem(gx + (dx + n_gx), n_gx) if dx else gx
        y = lax.rem(gy + (dy + n_gy), n_gy) if dy else gy
        return x, y

    size1, size2 = n_gx * 4, n_gy // 4
    me1 = gx * 4 + lax.rem(gy, 4)
    me2 = lax.div(gy, 4)

    def partner1(step):
        other = lax.rem(me1 + step, size1)
        return lax.div(other, 4), me2 * 4 + lax.rem(other, 4)

    def partner2(step):
        other = lax.rem(me2 + step, size2)
        return gx, other * 4 + lax.rem(gy, 4)

    barrier = pltpu.get_barrier_semaphore()
    for dx, dy in SIDES:
        pl.semaphore_signal(barrier, inc=1, device_id=device(dx, dy), device_id_type=MESH)

    loads = [
        pltpu.make_async_copy(storage_hbm, sa.at[:, OWN : OWN + CX], local_sem.at[0]),
        pltpu.make_async_copy(ids_hbm, ia.at[OWN : OWN + CX], local_sem.at[1]),
        pltpu.make_async_copy(source_hbm, source, local_sem.at[2]),
        pltpu.make_async_copy(bc_hbm, bc_ref, local_sem.at[3]),
        pltpu.make_async_copy(props_hbm, props_ref, local_sem.at[4]),
    ]
    for copy in loads:
        copy.start()

    loads[3].wait()
    own_bc = jnp.concatenate(
        [bc_ref[...].astype(jnp.float32), jnp.zeros((8, 112), jnp.float32)], axis=1
    )
    ba[1] = own_bc
    for slot in range(2):
        for field in range(2):
            for tile in range(2):
                z[slot, field, tile, 0] = zero
                z[slot, field, tile, EX - 1] = zero
    for field in range(2):
        for p in list(range(0, OWN)) + list(range(OWN + CX, EX)):
            rhs[field, p] = zero

    loads[1].wait()
    loads[4].wait()

    def table(row):
        line = jnp.broadcast_to(props_ref[row : row + 1, :], (8, 16))
        return jnp.concatenate([line, jnp.zeros((8, 112), jnp.float32)], axis=1)

    tab_p, tab_t, tab_e = jnp.sqrt(table(0)), jnp.sqrt(table(1)), table(2)

    def look(tab, ids):
        return jnp.take_along_axis(tab, ids, axis=1, mode="promise_in_bounds")

    def look_own(p):
        for f, tab in enumerate((tab_p, tab_t)):
            ga[f, p] = look(tab, ia[p])
        ea[p] = look(tab_e, ia[p])

    planes(OWN, OWN + CX, 16, lambda p: [look_own(p + i) for i in range(16)])
    pl.semaphore_wait(barrier, len(SIDES))

    first = []

    def push(src, dst, dx, dy):
        n = len(first)
        copy = pltpu.make_async_remote_copy(
            src_ref=src,
            dst_ref=dst,
            send_sem=s1.at[n],
            recv_sem=r1.at[n],
            device_id=device(dx, dy),
            device_id_type=MESH,
        )
        copy.start()
        first.append(copy)

    for dx, dy in SIDES:
        src_x = {0: slice(5, 21), 1: slice(16, 21), -1: slice(5, 10)}[dx]
        dst_x = {0: slice(5, 21), 1: slice(0, 5), -1: slice(21, 26)}[dx]
        y = {0: slice(0, 8), 1: slice(3, 8), -1: slice(0, 5)}[dy]
        half = {0: slice(0, 8), 1: slice(4, 8), -1: slice(0, 4)}[dy]
        place = {0: 1, 1: 0, -1: 2}[dx]
        push(ia.at[src_x, y, :], {0: ia, 1: ip, -1: inn}[dy].at[dst_x, y, :], dx, dy)
        push(ba.at[1, half, :], (bb if dy else ba).at[place, half, :], dx, dy)
    n_ids = len(first)
    loads[0].wait()
    for dx, dy in SIDES[4:6] + SIDES[:4] + SIDES[6:]:
        src_x = {0: slice(5, 21), 1: slice(17, 21), -1: slice(5, 9)}[dx]
        dst_x = {0: slice(5, 21), 1: slice(1, 5), -1: slice(21, 25)}[dx]
        half = {0: slice(0, 8), 1: slice(4, 8), -1: slice(0, 4)}[dy]
        push(sa.at[:, src_x, half, :], (sb if dy else sa).at[:, dst_x, half, :], dx, dy)

    has_n = (gy < n_gy - 1).astype(jnp.float32)
    has_p = (gy > 0).astype(jnp.float32)

    def tell(turn, reach):
        for way in (reach, -reach):
            pl.semaphore_signal(
                heard.at[turn], inc=1, device_id=device(0, way), device_id_type=MESH
            )

    has_w = (gx > 0).astype(jnp.float32)
    has_e = (gx < n_gx - 1).astype(jnp.float32)
    inside_b = jnp.where(rows < 4, has_n, has_p)

    for copy in first[:n_ids]:
        copy.wait_recv()

    def gather(p):
        inside = ((p >= OWN) | (gx > 0)) & ((p < OWN + CX) | (gx < n_gx - 1))
        inside = inside.astype(jnp.float32)
        id_n, id_p = inn[p], ip[p]
        for f, tab in enumerate((tab_p, tab_t)):
            n_tile = look(tab, id_n) * (inside * has_n)
            p_tile = look(tab, id_p) * (inside * has_p)
            gn[f, p] = n_tile
            gp[f, p] = p_tile
            gb[f, p] = jnp.where(rows < 4, n_tile, p_tile)
        eb[p] = jnp.where(rows < 4, look(tab_e, id_n), look(tab_e, id_p))

    def look_beside(p, inside):
        for f, tab in enumerate((tab_p, tab_t)):
            ga[f, p] = look(tab, ia[p]) * inside
        ea[p] = look(tab_e, ia[p])

    for p in range(OWN):
        look_beside(p, has_w)
        look_beside(p + OWN + CX, has_e)
    planes(0, EX, 26, lambda p: [gather(p + i) for i in range(26)])

    loads[2].wait()

    def inverse(g_p, g_t, e, lap_p, lap_t, sto):
        sp, spt, stp, st = sto
        first_ = sp + lap_p
        last = st + lap_t
        cross = stp + e * lap_p
        det = 1.0 / (first_ * last - cross * spt)
        k11 = g_p * (last - e * spt) * det
        k12 = g_p * (e * sp - stp) * det
        k21 = -(g_t * spt) * det
        k22 = g_t * first_ * det
        return k11, k12, k21, k22

    def diagonals(p):
        west = (p < OWN).astype(jnp.int32)
        east = (p >= OWN + CX).astype(jnp.int32)
        place = 1 - west + east
        shift = 127 - (p - OWN + 16 * west - 16 * east)
        top = lanes == 127
        bounds = [jnp.where(top, pltpu.roll(ref[place], shift, 1), 0.0) for ref in (ba, bb)]
        for f in range(2):
            a, b, n_tile, p_tile = ga[f, p], gb[f, p], gn[f, p], gp[f, p]
            a_up, a_down = pltpu.roll(a, 7, 0), pltpu.roll(a, 1, 0)
            b_up, b_down = pltpu.roll(b, 7, 0), pltpu.roll(b, 1, 0)
            y_a = jnp.where(rows == 7, b_up, a_up) + jnp.where(rows == 0, b_down, a_down)
            n_up, n_down = pltpu.roll(n_tile, 7, 0), pltpu.roll(n_tile, 1, 0)
            p_up, p_down = pltpu.roll(p_tile, 7, 0), pltpu.roll(p_tile, 1, 0)
            up = jnp.where(rows < 4, n_up, jnp.where(rows == 7, a_up, p_up))
            down = jnp.where(rows < 4, jnp.where(rows == 0, a_down, n_down), p_down)
            y_b = up + down
            lap_a = a * (ga[f, p - 1] + ga[f, p + 1] + y_a + z_sum(a, lanes))
            lap_b = b * (gb[f, p - 1] + gb[f, p + 1] + y_b + z_sum(b, lanes))
            if f == 0:
                lap_a = lap_a + 2.0 * (a * a) * bounds[0]
                lap_b = lap_b + 2.0 * (b * b) * bounds[1]
            lap[f, 0, p] = lap_a
            lap[f, 1, p] = lap_b

    def invert(p, tile, own):
        g_ref, e_ref, s_ref = ((ga, ea, sa), (gb, eb, sb))[tile]
        g_p, g_t, e = g_ref[0, p], g_ref[1, p], e_ref[p]
        sto = [s_ref[i, p] for i in range(4)]
        k11, k12, k21, k22 = inverse(g_p, g_t, e, lap[0, tile, p], lap[1, tile, p], sto)
        m[0, tile, p] = k11 * g_p
        m[1, tile, p] = k12 * g_t
        m[2, tile, p] = k21 * g_p
        m[3, tile, p] = k22 * g_t
        if own:
            x = p - OWN
            for i, value in enumerate((k11, k12, k21, k22)):
                k_own[i, x] = value
            recip[0, x] = 1.0 / g_p
            recip[1, x] = 1.0 / g_t
            u, t = source[0, x], source[1, x]
            rhs[0, p] = k11 * u + k12 * t
            rhs[1, p] = k21 * u + k22 * t

    planes(1, EX - 1, 24, lambda p: [diagonals(p + i) for i in range(24)])
    planes(OWN, OWN + CX, 8, lambda p: [invert(p + i, 0, True) for i in range(8)])
    for copy in first[n_ids:]:
        copy.wait_recv()
    tell(0, 2)
    planes(1, EX - 1, 24, lambda p: [invert(p + i, 1, False) for i in range(24)])
    planes(1, OWN, 4, lambda p: [invert(p + i, 0, False) for i in range(4)])
    planes(OWN + CX, EX - 1, 4, lambda p: [invert(p + i, 0, False) for i in range(4)])

    def solve():
        def start(p):
            for i in range(6):
                for f in range(2):
                    z[0, f, 0, p + i] = rhs[f, p + i]
                    z[0, f, 1, p + i] = zero

        planes(1, EX - 1, 6, start)

        def sweep(index, carry):
            old = lax.rem(index, 2)
            new = 1 - old

            def update(p):
                count = 24
                def load(f, i):
                    return [z[old, f, tile, p + i - 1] for tile in range(2)]

                for i in range(count):
                    sums = []
                    for f in range(2):
                        left, mid, right = load(f, i), load(f, i + 1), load(f, i + 2)
                        sums.append(ring_sum(left, mid[0], mid[1], right, rows, lanes))
                    for tile in range(2):
                        sum_q, sum_t = sums[0][tile], sums[1][tile]
                        for f in range(2):
                            value = (
                                m[2 * f, tile, p + i] * sum_q + m[2 * f + 1, tile, p + i] * sum_t
                            )
                            if tile == 0:
                                value = value + rhs[f, p + i]
                            z[new, f, tile, p + i] = value

            update(1)
            return carry

        lax.fori_loop(0, SWEEPS - 1, sweep, 0)

    last_slot = (SWEEPS - 1) % 2

    def exchange(turn, ssem, rsem):
        copies = []
        for dx, dy in SIDES:
            side = 0 if dx == 1 else 1
            wide = slice(20, 25) if dx == 1 else slice(1, 6)
            narrow = slice(21, 25) if dx == 1 else slice(1, 5)
            narrow_to = slice(1, 5) if dx == 1 else slice(0, 4)
            half = slice(0, 4) if dy == 1 else slice(4, 8)
            line = slice(7, 8) if dy == 1 else slice(0, 1)
            if dy == 0:
                moves = [(z.at[last_slot, :, 0, wide], rx.at[turn, side, :, 0])]
                for edge in (slice(0, 1), slice(7, 8)):
                    moves.append(
                        (
                            z.at[last_slot, :, 1, narrow, edge, :],
                            rx.at[turn, side, :, 1, narrow_to, edge, :],
                        )
                    )
            elif dx == 0:
                moves = [
                    (z.at[last_slot, :, 1, 4:22, half, :], rya.at[turn, :, :, half, :]),
                    (z.at[last_slot, :, 0, 5:21, line, :], ryb.at[turn, :, :, line, :]),
                ]
            else:
                moves = [
                    (z.at[last_slot, :, 1, wide, half, :], rca.at[turn, side, :, :, half, :]),
                    (z.at[last_slot, :, 0, narrow, line, :], rcb.at[turn, side, :, :, line, :]),
                ]
            for src, dst in moves:
                n = len(copies)
                copy = pltpu.make_async_remote_copy(
                    src_ref=src,
                    dst_ref=dst,
                    send_sem=ssem.at[turn, n],
                    recv_sem=rsem.at[turn, n],
                    device_id=device(dx, dy),
                    device_id_type=MESH,
                )
                copy.start()
                copies.append(copy)
        return copies

    def add_up(turn):
        def one(p, west, east):
            for f in range(2):
                a = z[last_slot, f, 0, p] + rya[turn, f, p - 4]
                b = z[last_slot, f, 1, p]
                if west:
                    a = a + (rx[turn, 0, f, 0, p - 4] + rca[turn, 0, f, p - 4])
                if east:
                    a = a + (rx[turn, 1, f, 0, p - 17] + rca[turn, 1, f, p - 17])
                if isinstance(p, int) and p == 4:
                    a = a * has_w
                if isinstance(p, int) and p == 21:
                    a = a * has_e
                fold[f, 0, p - 4] = a
                if not isinstance(p, int) or 5 <= p <= 20:
                    b = b + ryb[turn, f, p - 5]
                    if west:
                        b = b + (rx[turn, 0, f, 1, p - 4] + rcb[turn, 0, f, p - 5])
                    if east:
                        b = b + (rx[turn, 1, f, 1, p - 17] + rcb[turn, 1, f, p - 17])
                    fold[f, 1, p - 4] = b * inside_b

        for p in range(4, 9):
            one(p, True, False)
        planes(9, 17, 8, lambda p: [one(p + i, False, False) for i in range(8)])
        for p in range(17, 22):
            one(p, False, True)

    def apply(turn):
        def one(x, acc):
            i = x + 1
            sums, values = [], []
            for f in range(2):
                a, b = fold[f, 0, i], fold[f, 1, i]
                y_up = jnp.where(rows == 7, pltpu.roll(b, 7, 0), pltpu.roll(a, 7, 0))
                y_down = jnp.where(rows == 0, pltpu.roll(b, 1, 0), pltpu.roll(a, 1, 0))
                near = fold[f, 0, i - 1] + fold[f, 0, i + 1]
                sums.append(near + ((y_up + y_down) + z_sum(a, lanes)))
                values.append(a)
            p = x + OWN
            sp, spt, stp, st = [sa[j, p] for j in range(4)]
            q = values[0] * recip[0, x]
            t = values[1] * recip[1, x]
            u = q - ea[p] * t
            keep_p[turn][0, x] = u
            keep_p[turn][1, x] = t
            w_p = sp * u + lap[0, 0, p] * q + stp * t - ga[0, p] * sums[0]
            w_t = spt * u + (st + lap[1, 0, p]) * t - ga[1, p] * sums[1]
            src_p, src_t = source[0, x], source[1, x]
            if turn == 0:
                d_p, d_t = w_p - src_p, w_t - src_t
                rhs[0, p] = k_own[0, x] * d_p + k_own[1, x] * d_t
                rhs[1, p] = k_own[2, x] * d_p + k_own[3, x] * d_t
                terms = [(src_p, src_t, src_p, src_t), (src_p, src_t, d_p, d_t), (d_p, d_t, d_p, d_t)]
            else:
                o_p, o_t = keep_d[0][0, x], keep_d[0][1, x]
                d_p, d_t = w_p - o_p, w_t - o_t
                terms = [(src_p, src_t, d_p, d_t), (o_p, o_t, d_p, d_t), (d_p, d_t, d_p, d_t)]
            keep_d[turn][0, x] = d_p
            keep_d[turn][1, x] = d_t
            return tuple(
                total + (one_ * two + three * four)
                for total, (one_, three, two, four) in zip(acc, terms)
            )

        def group(index, acc):
            for i in range(16):
                acc = one(index * 16 + i, acc)
            return acc

        return lax.fori_loop(0, CX // 16, group, (zero, zero, zero))

    solve()
    copies = exchange(0, s2, r2)
    for copy in copies:
        copy.wait_recv()
    pl.semaphore_wait(heard.at[0], 2)
    tell(1, 4)
    add_up(0)
    dots_a = apply(0)
    for copy in copies:
        copy.wait_send()
    solve()
    copies = exchange(1, s2, r2)
    for copy in copies:
        copy.wait_recv()
    pl.semaphore_wait(heard.at[1], 2)
    tell(2, 8)
    add_up(1)
    dots_b = apply(1)

    ordered = [dots_a[0], dots_a[1], dots_b[0], dots_a[2], dots_b[1], dots_b[2]]
    tile = zero
    for i, part in enumerate(ordered):
        tile = jnp.where(rows == i, total_rows(part), tile)
    tile = total_rows(jnp.where(rows == lanes, total_lanes(tile), 0.0))[0:1]

    def all_sum(tile, box, me, size, partner, ssem, rsem):
        box[me] = tile

        def copy_of(step):
            return pltpu.make_async_remote_copy(
                src_ref=box.at[me],
                dst_ref=box.at[me],
                send_sem=ssem.at[step],
                recv_sem=rsem.at[step],
                device_id=partner(step),
                device_id_type=MESH,
            )

        def send(step, carry):
            copy_of(step).start()
            return carry

        def receive(step, carry):
            copy_of(step).wait_recv()
            return carry

        for step in range(1, size):
            send(step, 0)
        for step in range(1, size):
            receive(step, 0)
        parts = [box[i] for i in range(size)]
        while len(parts) > 1:
            parts = [parts[i] + parts[i + 1] for i in range(0, len(parts), 2)]
        return parts[0], copy_of

    tile, copy1 = all_sum(tile, g1, me1, size1, partner1, s3, r3)
    pl.semaphore_wait(heard.at[2], 2)
    tile, copy2 = all_sum(tile, g2, me2, size2, partner2, s4, r4)
    factors = small_problem(total_lanes(jnp.where(rows == lanes, tile, 0.0)), scale)
    table_out = zero
    for i, factor in enumerate(factors):
        table_out = jnp.where(rows == i, factor, table_out)
    factors_ref[...] = table_out

    def drain1(step, carry):
        copy1(step).wait_send()
        return carry

    def drain2(step, carry):
        copy2(step).wait_send()
        return carry

    for copy in first:
        copy.wait_send()
    for copy in copies:
        copy.wait_send()
    lax.fori_loop(1, size1, drain1, 0)
    lax.fori_loop(1, size2, drain2, 0)


def shards(adjoint_source, storage, soil_ids, bc_mask, soil_props):
    f32 = jnp.float32
    cells = 2.0 * 16 * lax.axis_size("gx") * 8 * lax.axis_size("gy") * 128
    out = pltpu.VMEM(adjoint_source.shape, f32)
    any_spec = pl.BlockSpec(memory_space=pltpu.HBM)
    vmem = pl.BlockSpec(memory_space=pltpu.VMEM)

    def buf(*lead, dtype=f32):
        return pltpu.VMEM(tuple(lead) + (8, 128), dtype)

    i32 = jnp.int32
    dma = pltpu.SemaphoreType.DMA
    p1, p2, d1, d2, factors = pl.pallas_call(
        functools.partial(kernel, math.sqrt(cells)),
        out_shape=(out, out, out, out, pltpu.VMEM((8, 128), f32)),
        in_specs=[any_spec] * 5,
        out_specs=(vmem,) * 5,
        scratch_shapes=[
            pltpu.VMEM((8, CX), i32), pltpu.VMEM((3, 16), f32),
            buf(2, CX),
            buf(4, EX), buf(4, EX),
            buf(EX, dtype=i32), buf(EX, dtype=i32), buf(EX, dtype=i32),
            buf(3), buf(3),
            buf(2, EX), buf(2, EX), buf(2, EX), buf(2, EX),
            buf(EX), buf(EX),
            buf(4, 2, EX),
            buf(4, CX), buf(2, 2, EX), buf(2, CX),
            buf(2, EX),
            buf(2, 2, 2, EX),
            buf(2, 2, 18),
            buf(2, 2, 18), buf(2, 2, 16),
            buf(2, 2, 2, 2, 5),
            buf(2, 2, 2, 5), buf(2, 2, 2, 4),
            pltpu.VMEM((32, 1, 128), f32), pltpu.VMEM((8, 1, 128), f32),
            dma((5,)), pltpu.SemaphoreType.REGULAR((3,)),
            dma((24,)), dma((24,)),
            dma((2, 18)), dma((2, 18)),
            dma((32,)), dma((32,)),
            dma((8,)), dma((8,)),
        ],
        compiler_params=pltpu.CompilerParams(
            collective_id=0, has_side_effects=True, vmem_limit_bytes=60 << 20
        ),
    )(adjoint_source, storage, soil_ids, bc_mask.T, soil_props)
    c = [factors[i] for i in range(8)]
    adjoint = c[0] * p1 + c[1] * p2
    residual = c[2] * adjoint_source + c[3] * d1 + c[4] * d2
    next_basis = c[5] * adjoint_source + c[6] * d1 + c[7] * d2
    return adjoint, residual, next_basis


def solution(mesh):
    in_specs = (
        P(None, "gx", "gy", None),
        P(None, "gx", "gy", None),
        P("gx", "gy", None),
        P("gx", "gy"),
        P(),
    )
    out_specs = (P(None, "gx", "gy", None), P(None, "gx", "gy", None), P(None, "gx", "gy", None))
    return jax.shard_map(shards, mesh=mesh, in_specs=in_specs, out_specs=out_specs, check_vma=False)
```

```python
import functools
import math

import jax
import jax.numpy as jnp
from jax import lax
from jax.experimental import pallas as pl
from jax.experimental.pallas import tpu as pltpu
from jax.sharding import PartitionSpec as P

MESH = pl.DeviceIdType.MESH
CX = 16
EX = 26
OWN = 5
SWEEPS = 6
epsilon = 1e-06


SIDES = [(1, 1), (1, -1), (-1, 1), (-1, -1), (0, 1), (0, -1), (1, 0), (-1, 0)]


def planes(low, high, chunk, body):
    count = (high - low) // chunk

    def group(index, carry):
        body(low + index * chunk)
        return carry

    lax.fori_loop(0, count, group, 0)


def ring_sum(left, a, b, right, rows, lanes):
    a_up, b_up = pltpu.roll(a, 7, 0), pltpu.roll(b, 7, 0)
    a_down, b_down = pltpu.roll(a, 1, 0), pltpu.roll(b, 1, 0)
    y_a = jnp.where(rows == 7, b_up, a_up) + jnp.where(rows == 0, b_down, a_down)
    b_high = jnp.where(rows == 7, a_up, jnp.where(rows == 3, 0.0, b_up))
    b_low = jnp.where(rows == 0, a_down, jnp.where(rows == 4, 0.0, b_down))
    y_b = b_high + b_low
    out_a = (left[0] + right[0]) + (y_a + z_sum(a, lanes))
    out_b = (left[1] + right[1]) + (y_b + z_sum(b, lanes))
    return out_a, out_b


def z_sum(tile, lanes):
    below = jnp.where(lanes == 0, 0.0, pltpu.roll(tile, 1, 1))
    above = jnp.where(lanes == 127, 0.0, pltpu.roll(tile, 127, 1))
    return below + above


def total_rows(tile):
    tile = tile + pltpu.roll(tile, 4, 0)
    tile = tile + pltpu.roll(tile, 2, 0)
    return tile + pltpu.roll(tile, 1, 0)


def total_lanes(tile):
    for shift in (64, 32, 16, 8, 4, 2, 1):
        tile = tile + pltpu.roll(tile, shift, 1)
    return tile


def small_problem(gram, size):
    ss, s1, s2, d11, d12, d22 = [gram[i : i + 1] for i in range(6)]
    square = ss + epsilon
    beta = jnp.sqrt(square)
    g1 = (epsilon - s1) / square
    h11 = 1.0 - g1
    norm1 = (d11 + 2.0 * g1 * s1 + g1 * g1 * ss) / square
    h21 = jnp.sqrt(jnp.maximum(norm1, 0.0) + epsilon)
    al = 1.0 / (beta * h21)
    ga = g1 * al
    h12 = (al * (s1 + s2) + ga * (ss + s1)) / beta
    v22 = al * al * d11 + 2.0 * al * ga * s1 + ga * ga * ss
    e22 = al * (al * d12 + ga * d11) + ga * (al * s2 + ga * s1)
    h22 = v22 + e22
    x3 = al
    x2 = ga + (1.0 - h22) * al
    x1 = (1.0 - h22) * ga - h12 / beta
    norm2 = (
        x3 * x3 * d22
        + x2 * x2 * d11
        + x1 * x1 * ss
        + 2.0 * (x3 * x2 * d12 + x3 * x1 * s2 + x2 * x1 * s1)
    )
    h32 = jnp.sqrt(jnp.maximum(norm2, 0.0) + epsilon)
    r1 = jnp.sqrt(h11 * h11 + h21 * h21)
    c1, n1 = h11 / r1, h21 / r1
    t0, t1 = c1 * beta, -n1 * beta
    u12 = c1 * h12 + n1 * h22
    low = c1 * h22 - n1 * h12
    r2 = jnp.sqrt(low * low + h32 * h32)
    c2 = low / r2
    y2 = c2 * t1 / r2
    y1 = (t0 - u12 * y2) / r1
    f1 = beta - h11 * y1 - h12 * y2
    f2 = -h21 * y1 - h22 * y2
    f3 = -h32 * y2
    a1, a2 = y1 / beta + y2 * ga, y2 * al
    inv = 1.0 / h32
    v31, v32, v33 = x1 * inv, x2 * inv, x3 * inv
    q1 = f1 / beta + f2 * ga + f3 * v31
    q2 = f2 * al + f3 * v32
    q3 = f3 * v33
    return a1, a2, q1, q2, q3, v31 * size, v32 * size, v33 * size


def kernel(
    scale,
    source_hbm, storage_hbm, ids_hbm, bc_hbm, props_hbm,
    p1, p2, d1, d2, factors_ref,
    bc_ref, props_ref, source, sa, sb, ia, inn, ip, ba, bb,
    ga, gb, gn, gp, ea, eb, m, k_own, lap, recip, rhs, z, fold,
    rya, ryb, rx, rca, rcb, g1, g2,
    local_sem, heard, s1, r1, s2, r2, s3, r3, s4, r4,
):
    gx, gy = lax.axis_index("gx"), lax.axis_index("gy")
    n_gx, n_gy = lax.axis_size("gx"), lax.axis_size("gy")
    rows = lax.broadcasted_iota(jnp.int32, (8, 128), 0)
    lanes = lax.broadcasted_iota(jnp.int32, (8, 128), 1)
    zero = jnp.zeros((8, 128), jnp.float32)
    keep_p, keep_d = (p1, p2), (d1, d2)

    def device(dx, dy):
        x = lax.rem(gx + (dx + n_gx), n_gx) if dx else gx
        y = lax.rem(gy + (dy + n_gy), n_gy) if dy else gy
        return x, y

    size1, size2 = n_gx * 4, n_gy // 4
    me1 = gx * 4 + lax.rem(gy, 4)
    me2 = lax.div(gy, 4)

    def partner1(step):
        other = lax.rem(me1 + step, size1)
        return lax.div(other, 4), me2 * 4 + lax.rem(other, 4)

    def partner2(step):
        other = lax.rem(me2 + step, size2)
        return gx, other * 4 + lax.rem(gy, 4)

    barrier = pltpu.get_barrier_semaphore()
    for dx, dy in SIDES:
        pl.semaphore_signal(barrier, inc=1, device_id=device(dx, dy), device_id_type=MESH)

    loads = [
        pltpu.make_async_copy(storage_hbm, sa.at[:, OWN : OWN + CX], local_sem.at[0]),
        pltpu.make_async_copy(ids_hbm, ia.at[OWN : OWN + CX], local_sem.at[1]),
        pltpu.make_async_copy(source_hbm, source, local_sem.at[2]),
        pltpu.make_async_copy(bc_hbm, bc_ref, local_sem.at[3]),
        pltpu.make_async_copy(props_hbm, props_ref, local_sem.at[4]),
    ]
    for copy in loads:
        copy.start()

    loads[3].wait()
    own_bc = jnp.concatenate(
        [bc_ref[...].astype(jnp.float32), jnp.zeros((8, 112), jnp.float32)], axis=1
    )
    ba[1] = own_bc
    for slot in range(2):
        for field in range(2):
            for tile in range(2):
                z[slot, field, tile, 0] = zero
                z[slot, field, tile, EX - 1] = zero
    for field in range(2):
        for p in list(range(0, OWN)) + list(range(OWN + CX, EX)):
            rhs[field, p] = zero

    loads[1].wait()
    loads[4].wait()

    def table(row):
        line = jnp.broadcast_to(props_ref[row : row + 1, :], (8, 16))
        return jnp.concatenate([line, jnp.zeros((8, 112), jnp.float32)], axis=1)

    tab_p, tab_t, tab_e = jnp.sqrt(table(0)), jnp.sqrt(table(1)), table(2)

    def look(tab, ids):
        return jnp.take_along_axis(tab, ids, axis=1, mode="promise_in_bounds")

    def look_own(p):
        for f, tab in enumerate((tab_p, tab_t)):
            ga[f, p] = look(tab, ia[p])
        ea[p] = look(tab_e, ia[p])

    planes(OWN, OWN + CX, 16, lambda p: [look_own(p + i) for i in range(16)])
    pl.semaphore_wait(barrier, len(SIDES))

    first = []

    def push(src, dst, dx, dy):
        n = len(first)
        copy = pltpu.make_async_remote_copy(
            src_ref=src,
            dst_ref=dst,
            send_sem=s1.at[n],
            recv_sem=r1.at[n],
            device_id=device(dx, dy),
            device_id_type=MESH,
        )
        copy.start()
        first.append(copy)

    for dx, dy in SIDES:
        src_x = {0: slice(5, 21), 1: slice(16, 21), -1: slice(5, 10)}[dx]
        dst_x = {0: slice(5, 21), 1: slice(0, 5), -1: slice(21, 26)}[dx]
        y = {0: slice(0, 8), 1: slice(3, 8), -1: slice(0, 5)}[dy]
        half = {0: slice(0, 8), 1: slice(4, 8), -1: slice(0, 4)}[dy]
        place = {0: 1, 1: 0, -1: 2}[dx]
        push(ia.at[src_x, y, :], {0: ia, 1: ip, -1: inn}[dy].at[dst_x, y, :], dx, dy)
        push(ba.at[1, half, :], (bb if dy else ba).at[place, half, :], dx, dy)
    n_ids = len(first)
    loads[0].wait()
    for dx, dy in SIDES[4:6] + SIDES[:4] + SIDES[6:]:
        src_x = {0: slice(5, 21), 1: slice(17, 21), -1: slice(5, 9)}[dx]
        dst_x = {0: slice(5, 21), 1: slice(1, 5), -1: slice(21, 25)}[dx]
        half = {0: slice(0, 8), 1: slice(4, 8), -1: slice(0, 4)}[dy]
        push(sa.at[:, src_x, half, :], (sb if dy else sa).at[:, dst_x, half, :], dx, dy)

    has_n = (gy < n_gy - 1).astype(jnp.float32)
    has_p = (gy > 0).astype(jnp.float32)

    def tell(turn, reach):
        for way in (reach, -reach):
            pl.semaphore_signal(
                heard.at[turn], inc=1, device_id=device(0, way), device_id_type=MESH
            )

    has_w = (gx > 0).astype(jnp.float32)
    has_e = (gx < n_gx - 1).astype(jnp.float32)
    inside_b = jnp.where(rows < 4, has_n, has_p)

    for copy in first[:n_ids]:
        copy.wait_recv()

    def gather(p):
        inside = ((p >= OWN) | (gx > 0)) & ((p < OWN + CX) | (gx < n_gx - 1))
        inside = inside.astype(jnp.float32)
        id_n, id_p = inn[p], ip[p]
        for f, tab in enumerate((tab_p, tab_t)):
            n_tile = look(tab, id_n) * (inside * has_n)
            p_tile = look(tab, id_p) * (inside * has_p)
            gn[f, p] = n_tile
            gp[f, p] = p_tile
            gb[f, p] = jnp.where(rows < 4, n_tile, p_tile)
        eb[p] = jnp.where(rows < 4, look(tab_e, id_n), look(tab_e, id_p))

    def look_beside(p, inside):
        for f, tab in enumerate((tab_p, tab_t)):
            ga[f, p] = look(tab, ia[p]) * inside
        ea[p] = look(tab_e, ia[p])

    for p in range(OWN):
        look_beside(p, has_w)
        look_beside(p + OWN + CX, has_e)
    planes(0, EX, 26, lambda p: [gather(p + i) for i in range(26)])

    loads[2].wait()

    def inverse(g_p, g_t, e, lap_p, lap_t, sto):
        sp, spt, stp, st = sto
        first_ = sp + lap_p
        last = st + lap_t
        cross = stp + e * lap_p
        det = 1.0 / (first_ * last - cross * spt)
        k11 = g_p * (last - e * spt) * det
        k12 = g_p * (e * sp - stp) * det
        k21 = -(g_t * spt) * det
        k22 = g_t * first_ * det
        return k11, k12, k21, k22

    def diagonals(p):
        west = (p < OWN).astype(jnp.int32)
        east = (p >= OWN + CX).astype(jnp.int32)
        place = 1 - west + east
        shift = 127 - (p - OWN + 16 * west - 16 * east)
        top = lanes == 127
        bounds = [jnp.where(top, pltpu.roll(ref[place], shift, 1), 0.0) for ref in (ba, bb)]
        for f in range(2):
            a, b, n_tile, p_tile = ga[f, p], gb[f, p], gn[f, p], gp[f, p]
            a_up, a_down = pltpu.roll(a, 7, 0), pltpu.roll(a, 1, 0)
            b_up, b_down = pltpu.roll(b, 7, 0), pltpu.roll(b, 1, 0)
            y_a = jnp.where(rows == 7, b_up, a_up) + jnp.where(rows == 0, b_down, a_down)
            n_up, n_down = pltpu.roll(n_tile, 7, 0), pltpu.roll(n_tile, 1, 0)
            p_up, p_down = pltpu.roll(p_tile, 7, 0), pltpu.roll(p_tile, 1, 0)
            up = jnp.where(rows < 4, n_up, jnp.where(rows == 7, a_up, p_up))
            down = jnp.where(rows < 4, jnp.where(rows == 0, a_down, n_down), p_down)
            y_b = up + down
            lap_a = a * (ga[f, p - 1] + ga[f, p + 1] + y_a + z_sum(a, lanes))
            lap_b = b * (gb[f, p - 1] + gb[f, p + 1] + y_b + z_sum(b, lanes))
            if f == 0:
                lap_a = lap_a + 2.0 * (a * a) * bounds[0]
                lap_b = lap_b + 2.0 * (b * b) * bounds[1]
            lap[f, 0, p] = lap_a
            lap[f, 1, p] = lap_b

    def invert(p, tile, own):
        g_ref, e_ref, s_ref = ((ga, ea, sa), (gb, eb, sb))[tile]
        g_p, g_t, e = g_ref[0, p], g_ref[1, p], e_ref[p]
        sto = [s_ref[i, p] for i in range(4)]
        k11, k12, k21, k22 = inverse(g_p, g_t, e, lap[0, tile, p], lap[1, tile, p], sto)
        m[0, tile, p] = k11 * g_p
        m[1, tile, p] = k12 * g_t
        m[2, tile, p] = k21 * g_p
        m[3, tile, p] = k22 * g_t
        if own:
            x = p - OWN
            for i, value in enumerate((k11, k12, k21, k22)):
                k_own[i, x] = value
            recip[0, x] = 1.0 / g_p
            recip[1, x] = 1.0 / g_t
            u, t = source[0, x], source[1, x]
            rhs[0, p] = k11 * u + k12 * t
            rhs[1, p] = k21 * u + k22 * t

    planes(1, EX - 1, 24, lambda p: [diagonals(p + i) for i in range(24)])
    planes(OWN, OWN + CX, 8, lambda p: [invert(p + i, 0, True) for i in range(8)])
    for copy in first[n_ids:]:
        copy.wait_recv()
    tell(0, 2)
    planes(1, EX - 1, 24, lambda p: [invert(p + i, 1, False) for i in range(24)])
    planes(1, OWN, 4, lambda p: [invert(p + i, 0, False) for i in range(4)])
    planes(OWN + CX, EX - 1, 4, lambda p: [invert(p + i, 0, False) for i in range(4)])

    def solve():
        def start(p):
            for i in range(6):
                for f in range(2):
                    z[0, f, 0, p + i] = rhs[f, p + i]
                    z[0, f, 1, p + i] = zero

        planes(1, EX - 1, 6, start)

        def sweep(index, carry):
            old = lax.rem(index, 2)
            new = 1 - old

            def update(p):
                count = 24
                def load(f, i):
                    return [z[old, f, tile, p + i - 1] for tile in range(2)]

                for i in range(count):
                    sums = []
                    for f in range(2):
                        left, mid, right = load(f, i), load(f, i + 1), load(f, i + 2)
                        sums.append(ring_sum(left, mid[0], mid[1], right, rows, lanes))
                    for tile in range(2):
                        sum_q, sum_t = sums[0][tile], sums[1][tile]
                        for f in range(2):
                            value = (
                                m[2 * f, tile, p + i] * sum_q + m[2 * f + 1, tile, p + i] * sum_t
                            )
                            if tile == 0:
                                value = value + rhs[f, p + i]
                            z[new, f, tile, p + i] = value

            update(1)
            return carry

        lax.fori_loop(0, SWEEPS - 1, sweep, 0)

    last_slot = (SWEEPS - 1) % 2

    def exchange(turn, ssem, rsem):
        copies = []
        for dx, dy in SIDES:
            side = 0 if dx == 1 else 1
            wide = slice(20, 25) if dx == 1 else slice(1, 6)
            narrow = slice(21, 25) if dx == 1 else slice(1, 5)
            narrow_to = slice(1, 5) if dx == 1 else slice(0, 4)
            half = slice(0, 4) if dy == 1 else slice(4, 8)
            line = slice(7, 8) if dy == 1 else slice(0, 1)
            if dy == 0:
                moves = [(z.at[last_slot, :, 0, wide], rx.at[turn, side, :, 0])]
                for edge in (slice(0, 1), slice(7, 8)):
                    moves.append(
                        (
                            z.at[last_slot, :, 1, narrow, edge, :],
                            rx.at[turn, side, :, 1, narrow_to, edge, :],
                        )
                    )
            elif dx == 0:
                moves = [
                    (z.at[last_slot, :, 1, 4:22, half, :], rya.at[turn, :, :, half, :]),
                    (z.at[last_slot, :, 0, 5:21, line, :], ryb.at[turn, :, :, line, :]),
                ]
            else:
                moves = [
                    (z.at[last_slot, :, 1, wide, half, :], rca.at[turn, side, :, :, half, :]),
                    (z.at[last_slot, :, 0, narrow, line, :], rcb.at[turn, side, :, :, line, :]),
                ]
            for src, dst in moves:
                n = len(copies)
                copy = pltpu.make_async_remote_copy(
                    src_ref=src,
                    dst_ref=dst,
                    send_sem=ssem.at[turn, n],
                    recv_sem=rsem.at[turn, n],
                    device_id=device(dx, dy),
                    device_id_type=MESH,
                )
                copy.start()
                copies.append(copy)
        return copies

    def add_up(turn):
        def one(p, west, east):
            for f in range(2):
                a = z[last_slot, f, 0, p] + rya[turn, f, p - 4]
                b = z[last_slot, f, 1, p]
                if west:
                    a = a + (rx[turn, 0, f, 0, p - 4] + rca[turn, 0, f, p - 4])
                if east:
                    a = a + (rx[turn, 1, f, 0, p - 17] + rca[turn, 1, f, p - 17])
                if isinstance(p, int) and p == 4:
                    a = a * has_w
                if isinstance(p, int) and p == 21:
                    a = a * has_e
                fold[f, 0, p - 4] = a
                if not isinstance(p, int) or 5 <= p <= 20:
                    b = b + ryb[turn, f, p - 5]
                    if west:
                        b = b + (rx[turn, 0, f, 1, p - 4] + rcb[turn, 0, f, p - 5])
                    if east:
                        b = b + (rx[turn, 1, f, 1, p - 17] + rcb[turn, 1, f, p - 17])
                    fold[f, 1, p - 4] = b * inside_b

        for p in range(4, 9):
            one(p, True, False)
        planes(9, 17, 8, lambda p: [one(p + i, False, False) for i in range(8)])
        for p in range(17, 22):
            one(p, False, True)

    def apply(turn):
        def one(x, acc):
            i = x + 1
            sums, values = [], []
            for f in range(2):
                a, b = fold[f, 0, i], fold[f, 1, i]
                y_up = jnp.where(rows == 7, pltpu.roll(b, 7, 0), pltpu.roll(a, 7, 0))
                y_down = jnp.where(rows == 0, pltpu.roll(b, 1, 0), pltpu.roll(a, 1, 0))
                near = fold[f, 0, i - 1] + fold[f, 0, i + 1]
                sums.append(near + ((y_up + y_down) + z_sum(a, lanes)))
                values.append(a)
            p = x + OWN
            sp, spt, stp, st = [sa[j, p] for j in range(4)]
            q = values[0] * recip[0, x]
            t = values[1] * recip[1, x]
            u = q - ea[p] * t
            keep_p[turn][0, x] = u
            keep_p[turn][1, x] = t
            w_p = sp * u + lap[0, 0, p] * q + stp * t - ga[0, p] * sums[0]
            w_t = spt * u + (st + lap[1, 0, p]) * t - ga[1, p] * sums[1]
            src_p, src_t = source[0, x], source[1, x]
            if turn == 0:
                d_p, d_t = w_p - src_p, w_t - src_t
                rhs[0, p] = k_own[0, x] * d_p + k_own[1, x] * d_t
                rhs[1, p] = k_own[2, x] * d_p + k_own[3, x] * d_t
                terms = [(src_p, src_t, src_p, src_t), (src_p, src_t, d_p, d_t), (d_p, d_t, d_p, d_t)]
            else:
                o_p, o_t = keep_d[0][0, x], keep_d[0][1, x]
                d_p, d_t = w_p - o_p, w_t - o_t
                terms = [(src_p, src_t, d_p, d_t), (o_p, o_t, d_p, d_t), (d_p, d_t, d_p, d_t)]
            keep_d[turn][0, x] = d_p
            keep_d[turn][1, x] = d_t
            return tuple(
                total + (one_ * two + three * four)
                for total, (one_, three, two, four) in zip(acc, terms)
            )

        def group(index, acc):
            for i in range(16):
                acc = one(index * 16 + i, acc)
            return acc

        return lax.fori_loop(0, CX // 16, group, (zero, zero, zero))

    solve()
    copies = exchange(0, s2, r2)
    for copy in copies:
        copy.wait_recv()
    pl.semaphore_wait(heard.at[0], 2)
    tell(1, 4)
    add_up(0)
    dots_a = apply(0)
    for copy in copies:
        copy.wait_send()
    solve()
    copies = exchange(1, s2, r2)
    for copy in copies:
        copy.wait_recv()
    pl.semaphore_wait(heard.at[1], 2)
    tell(2, 8)
    add_up(1)
    dots_b = apply(1)

    ordered = [dots_a[0], dots_a[1], dots_b[0], dots_a[2], dots_b[1], dots_b[2]]
    tile = zero
    for i, part in enumerate(ordered):
        tile = jnp.where(rows == i, total_rows(part), tile)
    tile = total_rows(jnp.where(rows == lanes, total_lanes(tile), 0.0))[0:1]

    def all_sum(tile, box, me, size, partner, ssem, rsem):
        box[me] = tile

        def copy_of(step):
            return pltpu.make_async_remote_copy(
                src_ref=box.at[me],
                dst_ref=box.at[me],
                send_sem=ssem.at[step],
                recv_sem=rsem.at[step],
                device_id=partner(step),
                device_id_type=MESH,
            )

        def send(step, carry):
            copy_of(step).start()
            return carry

        def receive(step, carry):
            copy_of(step).wait_recv()
            return carry

        for step in range(1, size):
            send(step, 0)
        for step in range(1, size):
            receive(step, 0)
        parts = [box[i] for i in range(size)]
        while len(parts) > 1:
            parts = [parts[i] + parts[i + 1] for i in range(0, len(parts), 2)]
        return parts[0], copy_of

    tile, copy1 = all_sum(tile, g1, me1, size1, partner1, s3, r3)
    pl.semaphore_wait(heard.at[2], 2)
    tile, copy2 = all_sum(tile, g2, me2, size2, partner2, s4, r4)
    factors = small_problem(total_lanes(jnp.where(rows == lanes, tile, 0.0)), scale)
    table_out = zero
    for i, factor in enumerate(factors):
        table_out = jnp.where(rows == i, factor, table_out)
    factors_ref[...] = table_out

    def drain1(step, carry):
        copy1(step).wait_send()
        return carry

    def drain2(step, carry):
        copy2(step).wait_send()
        return carry

    for copy in first:
        copy.wait_send()
    for copy in copies:
        copy.wait_send()
    for step in range(1, size1):
        drain1(step, 0)
    for step in range(1, size2):
        drain2(step, 0)


def shards(adjoint_source, storage, soil_ids, bc_mask, soil_props):
    f32 = jnp.float32
    cells = 2.0 * 16 * lax.axis_size("gx") * 8 * lax.axis_size("gy") * 128
    out = pltpu.VMEM(adjoint_source.shape, f32)
    any_spec = pl.BlockSpec(memory_space=pltpu.HBM)
    vmem = pl.BlockSpec(memory_space=pltpu.VMEM)

    def buf(*lead, dtype=f32):
        return pltpu.VMEM(tuple(lead) + (8, 128), dtype)

    i32 = jnp.int32
    dma = pltpu.SemaphoreType.DMA
    p1, p2, d1, d2, factors = pl.pallas_call(
        functools.partial(kernel, math.sqrt(cells)),
        out_shape=(out, out, out, out, pltpu.VMEM((8, 128), f32)),
        in_specs=[any_spec] * 5,
        out_specs=(vmem,) * 5,
        scratch_shapes=[
            pltpu.VMEM((8, CX), i32), pltpu.VMEM((3, 16), f32),
            buf(2, CX),
            buf(4, EX), buf(4, EX),
            buf(EX, dtype=i32), buf(EX, dtype=i32), buf(EX, dtype=i32),
            buf(3), buf(3),
            buf(2, EX), buf(2, EX), buf(2, EX), buf(2, EX),
            buf(EX), buf(EX),
            buf(4, 2, EX),
            buf(4, CX), buf(2, 2, EX), buf(2, CX),
            buf(2, EX),
            buf(2, 2, 2, EX),
            buf(2, 2, 18),
            buf(2, 2, 18), buf(2, 2, 16),
            buf(2, 2, 2, 2, 5),
            buf(2, 2, 2, 5), buf(2, 2, 2, 4),
            pltpu.VMEM((32, 1, 128), f32), pltpu.VMEM((8, 1, 128), f32),
            dma((5,)), pltpu.SemaphoreType.REGULAR((3,)),
            dma((24,)), dma((24,)),
            dma((2, 18)), dma((2, 18)),
            dma((32,)), dma((32,)),
            dma((8,)), dma((8,)),
        ],
        compiler_params=pltpu.CompilerParams(
            collective_id=0, has_side_effects=True, vmem_limit_bytes=60 << 20
        ),
    )(adjoint_source, storage, soil_ids, bc_mask.T, soil_props)
    c = [factors[i] for i in range(8)]
    adjoint = c[0] * p1 + c[1] * p2
    residual = c[2] * adjoint_source + c[3] * d1 + c[4] * d2
    next_basis = c[5] * adjoint_source + c[6] * d1 + c[7] * d2
    return adjoint, residual, next_basis


def solution(mesh):
    in_specs = (
        P(None, "gx", "gy", None),
        P(None, "gx", "gy", None),
        P("gx", "gy", None),
        P("gx", "gy"),
        P(),
    )
    out_specs = (P(None, "gx", "gy", None), P(None, "gx", "gy", None), P(None, "gx", "gy", None))
    return jax.shard_map(shards, mesh=mesh, in_specs=in_specs, out_specs=out_specs, check_vma=False)
```
